128 devices in a mesh: row: 8 (over x_lo, y), col: 8 (over z, core), feat: 2 (over x_hi).
Axes of the slice: x: 4 (x_hi: 2, x_lo: 2; x = x_hi * 2 + x_lo), y: 4, z: 4, core: 2. Of those that a mesh axis runs over, the one named last changes fastest.
Arguments:
- points: bfloat16 [4, 8, 512, 1024], P(None, 'row', None, ('col', 'feat')), may hold values from -2 to 2
- point_noise: float32 [4, 8, 512], P(None, 'row'), may hold values from 0.1 to 1
Outputs:
- schur_tiles: float32 [4, 8, 512, 4, 8, 512], P(None, 'row', None, None, 'col', 'feat')
- trace_mean: float32 [], replicated
- log_diagonal: float32 [], replicated
The draws below stay inside these ranges and needn't reach their ends.
All inputs are finite; a program needn't handle non-finite values.
Results may differ from the reference program's by a relative error of at most 0.003.
Values may be sent and summed in bfloat16 or wider, within the bound.
A program may use at most 128 MiB of HBM per device.

```python
import math
import jax
import jax.numpy as jnp
from jax import lax

TILE = 512
FEATURES = 1024
TILES_DEV = 4
N_ROW = 8
N_COL = 8


def draw_points(key, part):
    key_values = jax.random.fold_in(key, 11)
    key_rough = jax.random.fold_in(key, 23)
    tile_count = TILES_DEV * N_ROW
    tile_index = (jnp.arange(TILES_DEV)[:, None] * N_ROW + jnp.arange(N_ROW)[None, :]).astype(jnp.float32)
    scale_level = 0.6 * jnp.power(3.0, tile_index / max(tile_count - 1, 1))
    roughness = jax.random.uniform(key_rough, (TILES_DEV, N_ROW, TILE, 1), jnp.float32, 0.7, 1.4)
    entries = jnp.clip(jax.random.normal(key_values, (TILES_DEV, N_ROW, TILE, FEATURES), jnp.float32), -4.0, 4.0)
    values = entries * scale_level[:, :, None, None] * roughness / math.sqrt(32.0)
    return values.astype(jnp.bfloat16)


def block_levels(key, shape, cuts, smallest, top_value):
    def one(position, shards_of):
        heights = jax.random.uniform(jax.random.fold_in(jax.random.fold_in(key, 6), position), (shards_of,), jnp.float32, smallest / len(cuts), top_value / len(cuts))
        return jnp.repeat(jnp.exp(heights), shape[position] // shards_of).reshape((-1,) + (1,) * (len(shape) - position - 1))

    gain = one(*cuts[0])
    for cut in cuts[1:]:
        gain = gain * one(*cut)
    return gain


def setup_inputs(seed: int = 0) -> dict:
    seeds = jax.random.split(jax.random.key(seed), 3)
    return {
        "points": draw_points(jax.random.fold_in(seeds[2], 71), 0),
        "point_noise": jnp.clip(jnp.exp(math.log(1.0) - 2.3025851 * jax.random.uniform(seeds[1], (TILES_DEV, N_ROW, TILE), jnp.float32) ** block_levels(seeds[1], (TILES_DEV, N_ROW, TILE), ((1, 8),), -0.2, 0.2)), 0.1, 1.0),
    }


def reference(points, point_noise):
    tile_count = TILES_DEV * N_ROW
    point_count = tile_count * TILE
    all_points = points.reshape(point_count, FEATURES)
    gram_full = jnp.dot(all_points.astype(jnp.float32), all_points.T.astype(jnp.float32), preferred_element_type=jnp.float32)
    gram_full = gram_full + jnp.diag(point_noise.reshape(point_count).astype(jnp.float32))
    factor = jnp.linalg.cholesky(gram_full[:TILE, :TILE])
    inverse = jax.scipy.linalg.solve_triangular(factor, jnp.eye(TILE, dtype=jnp.float32), lower=True)
    panel_rows = jnp.dot(gram_full[:, :TILE], inverse.T, precision=lax.Precision.HIGHEST)
    schur_part = gram_full - jnp.dot(panel_rows, panel_rows.T, precision=lax.Precision.HIGHEST)
    schur_part = schur_part.at[:, :TILE].set(panel_rows)
    tile_index = (jnp.arange(point_count, dtype=jnp.int32) // TILE).astype(jnp.int32)
    lower_mask = tile_index[:, None] >= tile_index[None, :]
    schur_part = jnp.where(lower_mask, schur_part, jnp.float32(0.0))
    diagonal = jnp.diagonal(schur_part)[TILE:]
    trace_mean = jnp.sum(diagonal) / jnp.float32(point_count - TILE)
    log_diagonal = 2.0 * jnp.sum(jnp.log(jnp.diagonal(factor)))
    schur_tiles = schur_part.reshape(TILES_DEV, N_ROW, TILE, TILES_DEV, N_COL, TILE)
    return (schur_tiles, trace_mean, log_diagonal)
```

```python
import jax
import jax.numpy as jnp
from jax import lax
from jax.experimental import pallas as pl
from jax.experimental.pallas import tpu as pltpu
from jax.sharding import Mesh
from jax.sharding import PartitionSpec as P

F32 = jnp.float32
BF16 = jnp.bfloat16
HIGHEST = lax.Precision.HIGHEST
IDS = pl.DeviceIdType.MESH
AXES = ("x_lo", "y", "z", "core", "x_hi")
ROW = ("x_lo", "y")
COL = ("z", "core")
VMEM = pl.BlockSpec(memory_space=pltpu.VMEM)
ANY = pl.BlockSpec(memory_space=pl.ANY)
VMEM_LIMIT = 60 * 1024 * 1024


def factor_block(block):
    lane = lax.broadcasted_iota(jnp.int32, (8, 128), 1)
    sub = lax.broadcasted_iota(jnp.int32, (8, 128), 0)
    rows, logs = [], jnp.zeros((8, 128), F32)
    top, below = block[:8], block[8:]
    for k in range(16):
        c, n = 8 * k, 120 - 8 * k
        diag = [jnp.broadcast_to(top[:, c + t : c + t + 1], (8, 128)) for t in range(8)]
        here = (lane >= c) & (lane < c + 8)
        top = jnp.where(here, jnp.where(lane - c == sub, 1.0, 0.0), top)
        if n:
            cols = [jnp.broadcast_to(below[:, c + t : c + t + 1], (n, 128)) for t in range(8)]
            wide = lax.broadcasted_iota(jnp.int32, (n, 128), 1)
            below = jnp.where((wide >= c) & (wide < c + 8), 0.0, below)
        pivots = jnp.zeros((8, 128), F32)
        for t in range(8):
            pivot = diag[t][t : t + 1, :]
            inv = 1.0 / pivot
            pivots = jnp.where(sub == t, pivot, pivots)
            factor = jnp.where(sub > t, diag[t] * inv, 0.0)
            row = top[t : t + 1, :]
            ends = [diag[j][t : t + 1, :] for j in range(8)]
            for j in range(t + 1, 8):
                diag[j] = diag[j] - factor * ends[j]
            top = top - factor * row
            if n:
                scaled = cols[t] * inv
                below = below - scaled * row
                for j in range(t + 1, 8):
                    cols[j] = cols[j] - scaled * ends[j]
        rows.append(jnp.where(lane < c + 8, top, 0.0) * lax.rsqrt(pivots))
        logs = logs + jnp.log(pivots)
        if n:
            top, below = below[:8], below[8:]
    return jnp.concatenate(rows, 0), logs


def factor_step(k, w_ref, log_ref):
    n = w_ref.shape[0]
    at = pl.ds(pl.multiple_of(k * 128, 128), 128)
    block, logs = factor_block(w_ref[at, at])
    log_ref[...] += logs
    row_block = lax.broadcasted_iota(jnp.int32, (n, 128), 0) // 128
    col_block = lax.broadcasted_iota(jnp.int32, (128, n), 1) // 128
    all_block = lax.broadcasted_iota(jnp.int32, (n, n), 1) // 128
    lead = jnp.dot(block, w_ref[at, :], precision=HIGHEST)
    lead = jnp.where(col_block == k, jnp.concatenate([block] * (n // 128), 1), lead)
    left = lax.dot_general(w_ref[:, at], block, (((1,), (1,)), ((), ())), precision=HIGHEST)
    left = jnp.where(row_block > k, left, 0.0)
    rest = jnp.where(all_block == k, 0.0, w_ref[...])
    w_ref[...] = rest - jnp.dot(left, lead, precision=HIGHEST)
    w_ref[at, :] = lead


def remote(src, dst, send, recv, to):
    return pltpu.make_async_remote_copy(
        src_ref=src, dst_ref=dst, send_sem=send, recv_sem=recv, device_id=to, device_id_type=IDS
    )


def gather_kernel(
    x_ref, s_ref,
    rows_out, cols_out, lead_out, leadt_out, w_ref, log_ref,
    lead, rows, cols, noise,
    local_sem, own_sem, out_sem, lead_send, lead_recv, noise_send, noise_recv, line_send, line_recv,
    swap_send, swap_recv, row_send, row_recv, rswap_send, rswap_recv, spread_send, spread_recv, col_send, col_recv,
):
    a, b, z, k, h = (lax.axis_index(name) for name in AXES)
    q_line = z * 2 + h
    q_plane = b * 2 + a
    partner = {"core": 1 - k}

    def plane(d):
        return {"x_lo": (a + d // 4) % 2, "y": (b + d % 4) % 4}

    def line(d):
        return {"x_hi": (h + d // 4) % 2, "z": (z + d % 4) % 4}

    row_group = a * 4 + b
    to_z, to_k = row_group // 2, row_group % 2
    col_group = z * 2 + k
    from_a, from_b = col_group // 4, col_group % 4

    def spread_to(f):
        return {"x_lo": h, "y": z, "z": to_z, "core": to_k, "x_hi": f}

    def spread_self(f):
        return (a == h) & (b == z) & (z == to_z) & (k == to_k) & (h == f)

    def spread_from(kk):
        return {"x_lo": from_a, "y": from_b, "z": b, "core": kk, "x_hi": a}

    def from_self(kk):
        return (a == from_a) & (b == from_b) & (z == b) & (k == kk) & (h == a)

    own_row = pltpu.make_async_copy(x_ref, rows.at[q_line, k], own_sem)
    own_row.start()

    barrier = pltpu.get_barrier_semaphore()
    for d in range(1, 8):
        pl.semaphore_signal(barrier, inc=1, device_id=plane(d), device_id_type=IDS)
        pl.semaphore_signal(barrier, inc=1, device_id=line(d), device_id_type=IDS)
    pl.semaphore_signal(barrier, inc=1, device_id=partner, device_id_type=IDS)
    for i in range(2):
        @pl.when(jnp.logical_not(spread_self(i)))
        def _():
            pl.semaphore_signal(barrier, inc=1, device_id=spread_to(i), device_id_type=IDS)

        @pl.when(jnp.logical_not(from_self(i)))
        def _():
            pl.semaphore_signal(barrier, inc=1, device_id=spread_from(i), device_id_type=IDS)

    selfish = spread_self(0) | spread_self(1)

    @pl.when(selfish)
    def _():
        pl.semaphore_wait(barrier, 17)

    @pl.when(jnp.logical_not(selfish))
    def _():
        pl.semaphore_wait(barrier, 19)

    source = (a == 0) & (b == 0)

    @pl.when(source)
    def _():
        for d in range(1, 8):
            remote(x_ref.at[0], lead.at[q_line, k], lead_send.at[d - 1], lead_recv, plane(d)).start()
            remote(s_ref.at[0], noise, noise_send.at[d - 1], noise_recv, plane(d)).start()
        here = pltpu.make_async_copy(x_ref.at[0], lead.at[q_line, k], local_sem.at[0])
        there = pltpu.make_async_copy(s_ref.at[0], noise, local_sem.at[1])
        here.start()
        there.start()
        here.wait()
        there.wait()

    @pl.when(jnp.logical_not(source))
    def _():
        pltpu.make_async_copy(x_ref.at[0], lead.at[q_line, k], lead_recv).wait()
        pltpu.make_async_copy(s_ref.at[0], noise, noise_recv).wait()

    for d in range(1, 8):
        remote(
            lead.at[q_line, k], lead.at[q_line, k], line_send.at[d - 1], line_recv.at[q_line], line(d)
        ).start()
    for d in range(1, 8):
        q = ((z + d % 4) % 4) * 2 + (h + d // 4) % 2
        pltpu.make_async_copy(lead.at[q, k], lead.at[q, k], line_recv.at[q]).wait()
    swap = remote(lead.at[:, k], lead.at[:, k], swap_send, swap_recv, partner)
    swap.start()

    def row_piece(q, slot, to):
        return remote(rows.at[q, k], rows.at[q, k], row_send.at[slot], row_recv.at[q], to)

    def row_wait(q):
        pltpu.make_async_copy(rows.at[q, k], rows.at[q, k], row_recv.at[q]).wait()

    def col_piece(q, slot, to):
        return remote(cols.at[q], cols.at[q], col_send.at[slot], col_recv.at[q], to)

    def col_wait(q):
        pltpu.make_async_copy(cols.at[q], cols.at[q], col_recv.at[q]).wait()

    up_z, down_z = {"z": (z + 1) % 4}, {"z": (z + 3) % 4}
    up_y, down_y = {"y": (b + 1) % 4}, {"y": (b + 3) % 4}
    q_pair = z * 2 + 1 - h
    q_cross = b * 2 + 1 - a

    own_row.wait()
    row_piece(q_line, 0, {"x_hi": 1 - h}).start()
    row_piece(q_line, 1, up_z).start()
    row_piece(q_line, 2, down_z).start()
    for f in range(2):
        half = x_ref.at[:, :, f * 256 : f * 256 + 256]
        place = cols.at[q_line, k]

        @pl.when(spread_self(f))
        def _():
            pltpu.make_async_copy(half, place, spread_recv.at[k]).start()

        @pl.when(jnp.logical_not(spread_self(f)))
        def _():
            remote(half, place, spread_send.at[f], spread_recv.at[k], spread_to(f)).start()

    pltpu.make_async_copy(lead.at[:, k], lead.at[:, k], swap_recv).wait()
    for q in range(8):
        for kk in range(2):
            part = (q * 2 + kk) * 64
            leadt_out[part : part + 64, :] = lead[q, kk]
    lead_out[...] = leadt_out[...].T
    diag = lax.broadcasted_iota(jnp.int32, (128, 128), 0) == lax.broadcasted_iota(jnp.int32, (128, 128), 1)
    for i in range(4):
        block = slice(i * 128, i * 128 + 128)
        w_ref[block, :] = jnp.dot(lead_out[block, :], leadt_out[...], preferred_element_type=F32)
        w_ref[block, block] += jnp.where(diag, noise[i : i + 1, :], 0.0)
    log_ref[...] = jnp.zeros_like(log_ref)

    def step(i, carry):
        factor_step(i, w_ref, log_ref)

        @pl.when(i == 0)
        def _():
            for kk in range(2):
                q = q_plane
                pltpu.make_async_copy(cols.at[q, kk], cols.at[q, kk], spread_recv.at[kk]).wait()
            col_piece(q_plane, 0, {"x_lo": 1 - a}).start()
            col_piece(q_plane, 1, up_y).start()
            col_piece(q_plane, 2, down_y).start()
            row_wait(q_pair)
            row_piece(q_pair, 3, up_z).start()
            row_piece(q_pair, 4, down_z).start()

        @pl.when(i == 1)
        def _():
            col_wait(q_cross)
            col_piece(q_cross, 3, up_y).start()
            col_piece(q_cross, 4, down_y).start()
            for j in range(2):
                row_wait(((z + 3) % 4) * 2 + j)
                row_wait(((z + 1) % 4) * 2 + j)
            row_piece(((z + 3) % 4) * 2, 5, up_z).start()
            row_piece(((z + 1) % 4) * 2 + 1, 6, down_z).start()

        @pl.when(i == 2)
        def _():
            for j in range(2):
                col_wait(((b + 3) % 4) * 2 + j)
                col_wait(((b + 1) % 4) * 2 + j)
            col_piece(((b + 3) % 4) * 2, 5, up_y).start()
            col_piece(((b + 1) % 4) * 2 + 1, 6, down_y).start()
            row_wait(((z + 2) % 4) * 2)
            row_wait(((z + 2) % 4) * 2 + 1)
            remote(rows.at[:, k], rows.at[:, k], rswap_send, rswap_recv, partner).start()

        return carry

    lax.fori_loop(0, 4, step, 0)
    n = w_ref.shape[0]
    lower = lax.broadcasted_iota(jnp.int32, (n, n), 0) >= lax.broadcasted_iota(jnp.int32, (n, n), 1)
    w_ref[...] = jnp.where(lower, w_ref[...], 0.0)

    col_wait(((b + 2) % 4) * 2)
    col_wait(((b + 2) % 4) * 2 + 1)
    put_cols = pltpu.make_async_copy(cols, cols_out, out_sem.at[0])
    put_cols.start()
    pltpu.make_async_copy(rows.at[:, k], rows.at[:, k], rswap_recv).wait()
    put_rows = pltpu.make_async_copy(rows, rows_out, out_sem.at[1])
    put_rows.start()

    @pl.when(source)
    def _():
        for d in range(1, 8):
            remote(x_ref.at[0], lead.at[q_line, k], lead_send.at[d - 1], lead_recv, plane(d)).wait_send()
            remote(s_ref.at[0], noise, noise_send.at[d - 1], noise_recv, plane(d)).wait_send()

    for d in range(1, 8):
        remote(
            lead.at[q_line, k], lead.at[q_line, k], line_send.at[d - 1], line_recv.at[q_line], line(d)
        ).wait_send()
    swap.wait_send()
    for i in range(7):
        row_piece(q_line, i, up_z).wait_send()
        col_piece(q_plane, i, up_y).wait_send()
    for f in range(2):
        @pl.when(jnp.logical_not(spread_self(f)))
        def _():
            half = x_ref.at[:, :, f * 256 : f * 256 + 256]
            remote(half, cols.at[q_line, k], spread_send.at[f], spread_recv.at[k], spread_to(f)).wait_send()

    remote(rows.at[:, k], rows.at[:, k], rswap_send, rswap_recv, partner).wait_send()
    put_cols.wait()
    put_rows.wait()


def gather(x, s):
    dma = pltpu.SemaphoreType.DMA
    return pl.pallas_call(
        gather_kernel,
        out_shape=(
            jax.ShapeDtypeStruct((8, 2, 4, 64, 512), BF16),
            jax.ShapeDtypeStruct((8, 2, 4, 64, 256), BF16),
            jax.ShapeDtypeStruct((512, 1024), BF16),
            jax.ShapeDtypeStruct((1024, 512), BF16),
            jax.ShapeDtypeStruct((512, 512), F32),
            jax.ShapeDtypeStruct((8, 128), F32),
        ),
        in_specs=[ANY, ANY],
        out_specs=(ANY, ANY, VMEM, VMEM, VMEM, VMEM),
        scratch_shapes=[
            pltpu.VMEM((8, 2, 64, 512), BF16),
            pltpu.VMEM((8, 2, 4, 64, 512), BF16),
            pltpu.VMEM((8, 2, 4, 64, 256), BF16),
            pltpu.VMEM((4, 128), F32),
            dma((2,)), dma, dma((2,)),
            dma((7,)), dma, dma((7,)), dma, dma((7,)), dma((8,)),
            dma, dma, dma((7,)), dma((8,)), dma, dma, dma((2,)), dma((2,)), dma((7,)), dma((8,)),
        ],
        compiler_params=pltpu.CompilerParams(
            collective_id=0, has_side_effects=True, vmem_limit_bytes=VMEM_LIMIT
        ),
        name="gather_factor",
    )(x, s)


def split(value):
    high = value.astype(BF16)
    return high, (value - high.astype(F32)).astype(BF16)


def dot(left, right):
    return jnp.dot(left, right, preferred_element_type=F32)


def schur_kernel(
    rows_ref, cols_ref, lead_ref, leadt_ref, w_ref, s_ref,
    out_ref, trace_ref,
    wt, points, high, low, col_high, col_low,
):
    l = pl.program_id(0)
    r = lax.axis_index(ROW)
    c = lax.axis_index(COL)
    f = lax.axis_index("x_hi")
    diag = lax.broadcasted_iota(jnp.int32, (512, 512), 0) == lax.broadcasted_iota(jnp.int32, (512, 512), 1)

    @pl.when(l == 0)
    def _():
        wt[...] = w_ref[...].T
        trace_ref[...] = jnp.zeros_like(trace_ref)
        for m in range(4):
            first = dot(lead_ref[...], cols_ref[:, :, m].reshape(1024, 256))
            col_high[m], col_low[m] = split(jnp.dot(w_ref[...], first, precision=HIGHEST))

    points[...] = rows_ref[...].reshape(1024, 512).T
    first = dot(points[...], leadt_ref[...])
    corner = (l == 0) & (r == 0)
    noise = s_ref[0]
    first = first + jnp.where(diag & corner, noise, 0.0)
    panel = jnp.dot(first, wt[...], precision=HIGHEST)
    high[...], low[...] = split(panel)

    @pl.when(jnp.logical_not(corner))
    def _():
        given = points[...].astype(F32)
        total = jnp.sum(given * given, axis=0, keepdims=True)
        minus = jnp.sum(panel * panel, axis=0, keepdims=True)
        total = total[:, :512] + total[:, 512:] + noise - minus
        trace_ref[...] += total

    near = lax.broadcasted_iota(jnp.int32, (512, 256), 0) == lax.broadcasted_iota(jnp.int32, (512, 256), 1) + f * 256
    for m in range(4):
        def put(value):
            for half in range(2):
                out_ref[pl.ds(m * 2 + half, 512, stride=8), :] = value[:, half * 128 : half * 128 + 128]

        is_panel = (c == 0) & (m == 0)
        inside = (l > m) | ((l == m) & (r >= c))

        @pl.when(is_panel)
        def _():
            for half in range(2):
                at = pl.ds(pl.multiple_of(f * 256 + half * 128, 128), 128)
                out_ref[pl.ds(m * 2 + half, 512, stride=8), :] = high[:, at].astype(F32) + low[:, at].astype(F32)

        @pl.when(inside & jnp.logical_not(is_panel))
        def _():
            value = dot(points[...], cols_ref[:, :, m].reshape(1024, 256))
            value = value - dot(high[...], col_high[m])
            value = value - dot(high[...], col_low[m])
            value = value - dot(low[...], col_high[m])
            here = noise[:, :256] * (f == 0).astype(F32) + noise[:, 256:] * (f == 1).astype(F32)
            put(value + jnp.where(near & (l == m) & (r == c), here, 0.0))

        @pl.when(jnp.logical_not(inside))
        def _():
            put(jnp.zeros((512, 256), F32))


def schur(rows, cols, lead, leadt, w, s):
    return pl.pallas_call(
        schur_kernel,
        grid=(4,),
        out_shape=(
            jax.ShapeDtypeStruct((4 * 512 * 8, 128), F32),
            jax.ShapeDtypeStruct((1, 512), F32),
        ),
        in_specs=[
            pl.BlockSpec((8, 2, None, 64, 512), lambda l: (0, 0, l, 0, 0)),
            VMEM, VMEM, VMEM, VMEM,
            pl.BlockSpec((1, 1, 512), lambda l: (l, 0, 0)),
        ],
        out_specs=(
            pl.BlockSpec((512 * 8, 128), lambda l: (l, 0)),
            pl.BlockSpec((1, 512), lambda l: (0, 0)),
        ),
        scratch_shapes=[
            pltpu.VMEM((512, 512), F32),
            pltpu.VMEM((512, 1024), BF16),
            pltpu.VMEM((512, 512), BF16),
            pltpu.VMEM((512, 512), BF16),
            pltpu.VMEM((4, 512, 256), BF16),
            pltpu.VMEM((4, 512, 256), BF16),
        ],
        compiler_params=pltpu.CompilerParams(vmem_limit_bytes=VMEM_LIMIT),
        name="schur",
    )(rows, cols, lead, leadt, w, s)


def shards(points, point_noise):
    x = jnp.swapaxes(points[:, 0], 1, 2)
    s = point_noise.reshape(4, 512)
    rows, cols, lead, leadt, w, logs = gather(x, s.reshape(4, 4, 128))
    out, trace = schur(rows, cols, lead, leadt, w, s.reshape(4, 1, 512))
    total = lax.psum(jnp.sum(trace), ROW)
    count = 32 * 512 - 512
    return out.reshape(4, 1, 512, 4, 1, 256), total / count, jnp.sum(logs[:, 0])


def solution(mesh):
    torus = Mesh(mesh.devices.reshape(2, 4, 4, 2, mesh.shape["feat"]), AXES)
    return jax.shard_map(
        shards,
        mesh=torus,
        in_specs=(P(None, ROW, None, ("z", "core", "x_hi")), P(None, ROW, None)),
        out_specs=(P(None, ROW, None, None, COL, "x_hi"), P(), P()),
        check_vma=False,
    )
```

```python
import jax
import jax.numpy as jnp
from jax import lax
from jax.experimental import pallas as pl
from jax.experimental.pallas import tpu as pltpu
from jax.sharding import Mesh
from jax.sharding import PartitionSpec as P

F32 = jnp.float32
BF16 = jnp.bfloat16
HIGHEST = lax.Precision.HIGHEST
IDS = pl.DeviceIdType.MESH
AXES = ("x_lo", "y", "z", "core", "x_hi")
ROW = ("x_lo", "y")
COL = ("z", "core")
VMEM = pl.BlockSpec(memory_space=pltpu.VMEM)
ANY = pl.BlockSpec(memory_space=pl.ANY)
VMEM_LIMIT = 60 * 1024 * 1024


def factor_block(block):
    lane = lax.broadcasted_iota(jnp.int32, (8, 128), 1)
    sub = lax.broadcasted_iota(jnp.int32, (8, 128), 0)
    rows, logs = [], jnp.zeros((8, 128), F32)
    top, below = block[:8], block[8:]
    for k in range(16):
        c, n = 8 * k, 120 - 8 * k
        diag = [jnp.broadcast_to(top[:, c + t : c + t + 1], (8, 128)) for t in range(8)]
        here = (lane >= c) & (lane < c + 8)
        top = jnp.where(here, jnp.where(lane - c == sub, 1.0, 0.0), top)
        if n:
            cols = [jnp.broadcast_to(below[:, c + t : c + t + 1], (n, 128)) for t in range(8)]
            wide = lax.broadcasted_iota(jnp.int32, (n, 128), 1)
            below = jnp.where((wide >= c) & (wide < c + 8), 0.0, below)
        pivots = jnp.zeros((8, 128), F32)
        for t in range(8):
            pivot = diag[t][t : t + 1, :]
            inv = 1.0 / pivot
            pivots = jnp.where(sub == t, pivot, pivots)
            factor = jnp.where(sub > t, diag[t] * inv, 0.0)
            row = top[t : t + 1, :]
            ends = [diag[j][t : t + 1, :] for j in range(8)]
            for j in range(t + 1, 8):
                diag[j] = diag[j] - factor * ends[j]
            top = top - factor * row
            if n:
                scaled = cols[t] * inv
                below = below - scaled * row
                for j in range(t + 1, 8):
                    cols[j] = cols[j] - scaled * ends[j]
        rows.append(jnp.where(lane < c + 8, top, 0.0) * lax.rsqrt(pivots))
        logs = logs + jnp.log(pivots)
        if n:
            top, below = below[:8], below[8:]
    return jnp.concatenate(rows, 0), logs


def factor_step(k, w_ref, log_ref, between):
    n = w_ref.shape[0]
    at = pl.ds(pl.multiple_of(k * 128, 128), 128)
    block, logs = factor_block(w_ref[at, at])
    log_ref[...] += logs
    between()
    row_block = lax.broadcasted_iota(jnp.int32, (n, 128), 0) // 128
    col_block = lax.broadcasted_iota(jnp.int32, (128, n), 1) // 128
    all_block = lax.broadcasted_iota(jnp.int32, (n, n), 1) // 128
    lead = jnp.dot(block, w_ref[at, :], precision=HIGHEST)
    lead = jnp.where(col_block == k, jnp.concatenate([block] * (n // 128), 1), lead)
    left = lax.dot_general(w_ref[:, at], block, (((1,), (1,)), ((), ())), precision=HIGHEST)
    left = jnp.where(row_block > k, left, 0.0)
    rest = jnp.where(all_block == k, 0.0, w_ref[...])
    w_ref[...] = rest - jnp.dot(left, lead, precision=HIGHEST)
    w_ref[at, :] = lead


def remote(src, dst, send, recv, to):
    return pltpu.make_async_remote_copy(
        src_ref=src, dst_ref=dst, send_sem=send, recv_sem=recv, device_id=to, device_id_type=IDS
    )


def gather_kernel(
    x_ref, s_ref,
    rows_out, cols_out, lead_out, leadt_out, w_ref, log_ref,
    lead, rows, cols, noise,
    own_sem, row_out, col_out, lead_send, lead_recv, noise_send, noise_recv, line_send, line_recv,
    swap_send, swap_recv, row_send, row_recv, rswap_send, rswap_recv, spread_send, spread_recv, col_send, col_recv,
):
    a, b, z, k, h = (lax.axis_index(name) for name in AXES)
    q_line = z * 2 + h
    partner = {"core": 1 - k}

    def plane(d):
        return {"x_lo": (a + d // 4) % 2, "y": (b + d % 4) % 4}

    def line(d):
        return {"x_hi": (h + d // 4) % 2, "z": (z + d % 4) % 4}

    row_group = a * 4 + b
    to_z, to_k = row_group // 2, row_group % 2
    to_a, to_b = (a + h) % 2, (b + z) % 4
    col_group = z * 2 + k
    from_a, from_b = col_group // 4, col_group % 4

    def spread_to(f):
        return {"x_lo": to_a, "y": to_b, "z": to_z, "core": to_k, "x_hi": f}

    def spread_self(f):
        return (a == to_a) & (b == to_b) & (z == to_z) & (k == to_k) & (h == f)

    def spread_from(kk):
        return {"x_lo": from_a, "y": from_b, "z": (b + 4 - from_b) % 4, "core": kk, "x_hi": (a + from_a) % 2}

    def from_self(kk):
        return (
            (a == from_a) & (b == from_b) & (z == (b + 4 - from_b) % 4) & (k == kk) & (h == (a + from_a) % 2)
        )

    def q_at(da, db):
        return ((b + db + 4 - from_b) % 4) * 2 + (a + da + from_a) % 2

    def q_on(j, db):
        return ((b + db + 4 - from_b) % 4) * 2 + (j + from_a) % 2

    q_plane = q_at(0, 0)

    own_row = pltpu.make_async_copy(x_ref, rows.at[q_line, k], own_sem)
    own_row.start()

    barrier = pltpu.get_barrier_semaphore()
    for d in range(1, 8):
        pl.semaphore_signal(barrier, inc=1, device_id=plane(d), device_id_type=IDS)
        pl.semaphore_signal(barrier, inc=1, device_id=line(d), device_id_type=IDS)
    pl.semaphore_signal(barrier, inc=1, device_id=partner, device_id_type=IDS)
    for i in range(2):
        @pl.when(jnp.logical_not(spread_self(i)))
        def _():
            pl.semaphore_signal(barrier, inc=1, device_id=spread_to(i), device_id_type=IDS)

        @pl.when(jnp.logical_not(from_self(i)))
        def _():
            pl.semaphore_signal(barrier, inc=1, device_id=spread_from(i), device_id_type=IDS)

    selfish = spread_self(0) | spread_self(1)

    @pl.when(selfish)
    def _():
        pl.semaphore_wait(barrier, 17)

    @pl.when(jnp.logical_not(selfish))
    def _():
        pl.semaphore_wait(barrier, 19)

    def row_piece(q, slot, to):
        src = x_ref if slot < 3 else rows.at[q, k]
        return remote(src, rows.at[q, k], row_send.at[slot], row_recv.at[q], to)

    def row_wait(q):
        pltpu.make_async_copy(rows.at[q, k], rows.at[q, k], row_recv.at[q]).wait()

    def col_piece(q, slot, to):
        return remote(cols.at[q], cols.at[q], col_send.at[slot], col_recv.at[q], to)

    def col_wait(q):
        pltpu.make_async_copy(cols.at[q], cols.at[q], col_recv.at[q]).wait()

    def put_col(q, slot):
        return pltpu.make_async_copy(cols.at[q], cols_out.at[q], col_out.at[slot])

    def put_row(kk, slot):
        return pltpu.make_async_copy(rows.at[:, kk], rows_out.at[:, kk], row_out.at[slot])

    up_z, down_z = {"z": (z + 1) % 4}, {"z": (z + 3) % 4}
    up_y, down_y = {"y": (b + 1) % 4}, {"y": (b + 3) % 4}
    q_pair = z * 2 + 1 - h
    q_cross = q_at(1, 0)

    root = b == 0
    source = root & (a == 0)

    def lead_part(i):
        return pl.ds(i * 32, 32)

    def lead_piece(i, d, to):
        part = lead_part(i)
        dst = lead.at[q_line, k, part]
        return remote(dst, dst, lead_send.at[i, d], lead_recv.at[i], to)

    def noise_piece(d, to):
        return remote(noise, noise, noise_send.at[d], noise_recv, to)

    @pl.when(source)
    def _():
        for i in range(2):
            pltpu.make_async_copy(x_ref.at[0, lead_part(i)], lead.at[q_line, k, lead_part(i)], lead_recv.at[i]).start()
        pltpu.make_async_copy(s_ref.at[0], noise, noise_recv).start()

    def lead_wait(i):
        part = lead.at[q_line, k, lead_part(i)]
        pltpu.make_async_copy(part, part, lead_recv.at[i]).wait()

        @pl.when(source)
        def _():
            lead_piece(i, 0, {"x_lo": 1 - a}).start()

        @pl.when(root)
        def _():
            for d in range(1, 4):
                lead_piece(i, d, {"y": (b + d) % 4}).start()

    def spread():
        for f in range(2):
            half = x_ref.at[:, :, f * 256 : f * 256 + 256]
            place = cols.at[q_line, k]

            @pl.when(spread_self(f))
            def _():
                pltpu.make_async_copy(half, place, spread_recv.at[k]).start()

            @pl.when(jnp.logical_not(spread_self(f)))
            def _():
                remote(half, place, spread_send.at[f], spread_recv.at[k], spread_to(f)).start()

    pl.when(jnp.logical_not(root))(spread)

    def line_piece(i, d):
        part = lead.at[q_line, k, lead_part(i)]
        return remote(part, part, line_send.at[i, d - 1], line_recv.at[i, q_line], line(d))

    for i in range(2):
        lead_wait(i)
        for d in range(1, 8):
            line_piece(i, d).start()
    pl.when(root)(spread)
    pltpu.make_async_copy(noise, noise, noise_recv).wait()

    @pl.when(source)
    def _():
        noise_piece(0, {"x_lo": 1 - a}).start()

    @pl.when(root)
    def _():
        for d in range(1, 4):
            noise_piece(d, {"y": (b + d) % 4}).start()

    for kk in range(2):
        pltpu.make_async_copy(cols.at[q_plane, kk], cols.at[q_plane, kk], spread_recv.at[kk]).wait()
    col_piece(q_plane, 1, up_y).start()
    col_piece(q_plane, 2, down_y).start()
    col_piece(q_plane, 0, {"x_lo": 1 - a}).start()

    for d in range(1, 8):
        q = ((z + d % 4) % 4) * 2 + (h + d // 4) % 2
        for i in range(2):
            part = lead.at[q, k, lead_part(i)]
            pltpu.make_async_copy(part, part, line_recv.at[i, q]).wait()
    swap = remote(lead.at[:, k], lead.at[:, k], swap_send, swap_recv, partner)
    swap.start()
    row_piece(q_line, 0, {"x_hi": 1 - h}).start()
    row_piece(q_line, 1, up_z).start()
    row_piece(q_line, 2, down_z).start()
    pltpu.make_async_copy(lead.at[:, k], lead.at[:, k], swap_recv).wait()
    for q in range(8):
        for kk in range(2):
            part = (q * 2 + kk) * 64
            leadt_out[part : part + 64, :] = lead[q, kk]
    lead_out[...] = leadt_out[...].T
    diag = lax.broadcasted_iota(jnp.int32, (128, 128), 0) == lax.broadcasted_iota(jnp.int32, (128, 128), 1)
    for i in range(4):
        block = slice(i * 128, i * 128 + 128)
        w_ref[block, :] = jnp.dot(lead_out[block, :], leadt_out[...], preferred_element_type=F32)
        w_ref[block, block] += jnp.where(diag, noise[i : i + 1, :], 0.0)
    log_ref[...] = jnp.zeros_like(log_ref)

    col_wait(q_cross)
    col_piece(q_cross, 3, up_y).start()
    col_piece(q_cross, 4, down_y).start()
    own_row.wait()

    def events(step):
        if step == 0:
            row_wait(q_pair)
            row_piece(q_pair, 3, up_z).start()
            row_piece(q_pair, 4, down_z).start()
        if step == 1:
            for j in range(2):
                col_wait(q_on(j, 3))
                col_wait(q_on(j, 1))
            col_piece(q_on(0, 3), 5, up_y).start()
            col_piece(q_on(1, 1), 6, down_y).start()
            for j in range(2):
                for d in range(3):
                    put_col(q_on(j, d + 3), d * 2 + j).start()
        if step == 3:
            for j in range(2):
                row_wait(((z + 3) % 4) * 2 + j)
                row_wait(((z + 1) % 4) * 2 + j)
            row_piece(((z + 3) % 4) * 2, 5, up_z).start()
            row_piece(((z + 1) % 4) * 2 + 1, 6, down_z).start()
        if step == 4:
            for j in range(2):
                col_wait(q_on(j, 2))
                put_col(q_on(j, 2), 6 + j).start()
        if step == 6:
            row_wait(((z + 2) % 4) * 2)
            row_wait(((z + 2) % 4) * 2 + 1)
            remote(rows.at[:, k], rows.at[:, k], rswap_send, rswap_recv, partner).start()
            put_row(k, 0).start()

    def step(i, carry):
        def between():
            for e in (0, 2, 3):
                pl.when(i == e)(lambda e=e: events(2 * e))

        factor_step(i, w_ref, log_ref, between)
        for e in (0, 1):
            pl.when(i == e)(lambda e=e: events(2 * e + 1))
        return carry

    lax.fori_loop(0, 4, step, 0)
    n = w_ref.shape[0]
    lower = lax.broadcasted_iota(jnp.int32, (n, n), 0) >= lax.broadcasted_iota(jnp.int32, (n, n), 1)
    w_ref[...] = jnp.where(lower, w_ref[...], 0.0)

    pltpu.make_async_copy(rows.at[:, k], rows.at[:, k], rswap_recv).wait()
    put_row(1 - k, 1).start()

    for i in range(2):
        @pl.when(source)
        def _():
            lead_piece(i, 0, partner).wait_send()

        @pl.when(root)
        def _():
            for d in range(1, 4):
                lead_piece(i, d, partner).wait_send()

        for d in range(1, 8):
            line_piece(i, d).wait_send()

    @pl.when(source)
    def _():
        noise_piece(0, partner).wait_send()

    @pl.when(root)
    def _():
        for d in range(1, 4):
            noise_piece(d, partner).wait_send()

    swap.wait_send()
    for i in range(7):
        row_piece(q_line, i, up_z).wait_send()
        col_piece(q_plane, i, up_y).wait_send()
    for f in range(2):
        @pl.when(jnp.logical_not(spread_self(f)))
        def _():
            half = x_ref.at[:, :, f * 256 : f * 256 + 256]
            remote(half, cols.at[q_line, k], spread_send.at[f], spread_recv.at[k], spread_to(f)).wait_send()

    remote(rows.at[:, k], rows.at[:, k], rswap_send, rswap_recv, partner).wait_send()
    for j in range(2):
        put_row(k, j).wait()
    for j in range(8):
        put_col(q_plane, j).wait()


def gather(x, s):
    dma = pltpu.SemaphoreType.DMA
    return pl.pallas_call(
        gather_kernel,
        out_shape=(
            jax.ShapeDtypeStruct((8, 2, 4, 64, 512), BF16),
            jax.ShapeDtypeStruct((8, 2, 4, 64, 256), BF16),
            jax.ShapeDtypeStruct((512, 1024), BF16),
            jax.ShapeDtypeStruct((1024, 512), BF16),
            jax.ShapeDtypeStruct((512, 512), F32),
            jax.ShapeDtypeStruct((8, 128), F32),
        ),
        in_specs=[ANY, ANY],
        out_specs=(ANY, ANY, VMEM, VMEM, VMEM, VMEM),
        scratch_shapes=[
            pltpu.VMEM((8, 2, 64, 512), BF16),
            pltpu.VMEM((8, 2, 4, 64, 512), BF16),
            pltpu.VMEM((8, 2, 4, 64, 256), BF16),
            pltpu.VMEM((4, 128), F32),
            dma, dma((2,)), dma((8,)),
            dma((2, 4)), dma((2,)), dma((4,)), dma, dma((2, 7)), dma((2, 8)),
            dma, dma, dma((7,)), dma((8,)), dma, dma, dma((2,)), dma((2,)), dma((7,)), dma((8,)),
        ],
        compiler_params=pltpu.CompilerParams(
            collective_id=0, has_side_effects=True, vmem_limit_bytes=VMEM_LIMIT
        ),
        name="gather_factor",
    )(x, s)


def split(value):
    high = value.astype(BF16)
    return high, (value - high.astype(F32)).astype(BF16)


def dot(left, right):
    return jnp.dot(left, right, preferred_element_type=F32)


def schur_kernel(
    rows_ref, cols_ref, lead_ref, leadt_ref, w_ref, s_ref,
    out_ref, trace_ref,
    wide, tall, left, right,
):
    l = pl.program_id(0)
    r = lax.axis_index(ROW)
    c = lax.axis_index(COL)
    f = lax.axis_index("x_hi")

    @pl.when(l == 0)
    def _():
        high, low = split(w_ref[...])
        wide[:, :512], wide[:, 512:1024], wide[:, 1024:] = high, low, high
        tall[...] = wide[...].T
        trace_ref[...] = jnp.zeros_like(trace_ref)
        for m in range(4):
            points = cols_ref[:, :, m].reshape(1024, 256)
            high, low = split(dot(lead_ref[...], points))
            high, low = split(-dot(wide[...], jnp.concatenate([high, high, low], 0)))
            right[m, :1024] = points
            right[m, 1024:1536], right[m, 1536:2048], right[m, 2048:] = high, low, high

    points = rows_ref[...].reshape(1024, 512).T
    left[:, :1024] = points
    first = dot(points, leadt_ref[...])
    corner = (l == 0) & (r == 0)
    noise = s_ref[0]
    diag = lax.broadcasted_iota(jnp.int32, (512, 512), 0) == lax.broadcasted_iota(jnp.int32, (512, 512), 1)
    first = first + jnp.where(diag & corner, noise, 0.0)
    high, low = split(first)
    panel = dot(jnp.concatenate([high, high, low], 1), tall[...])
    high, low = split(panel)
    left[:, 1024:1536], left[:, 1536:2048], left[:, 2048:] = high, high, low

    @pl.when(jnp.logical_not(corner))
    def _():
        given = points.astype(F32)
        total = jnp.sum(given * given, axis=0, keepdims=True)
        minus = jnp.sum(panel * panel, axis=0, keepdims=True)
        trace_ref[...] += total[:, :512] + total[:, 512:] + noise - minus

    near = lax.broadcasted_iota(jnp.int32, (512, 256), 0) == lax.broadcasted_iota(jnp.int32, (512, 256), 1) + f * 256
    for m in range(4):
        def put(value):
            for half in range(2):
                out_ref[pl.ds(m * 2 + half, 512, stride=8), :] = value[:, half * 128 : half * 128 + 128]

        is_panel = (c == 0) & (m == 0)
        inside = (l > m) | ((l == m) & (r > c))
        same = (l == m) & (r == c)

        def value():
            return dot(left[...], right[m])

        @pl.when(is_panel)
        def _():
            for half in range(2):
                high = left[:, pl.ds(pl.multiple_of(1024 + f * 256 + half * 128, 128), 128)]
                low = left[:, pl.ds(pl.multiple_of(2048 + f * 256 + half * 128, 128), 128)]
                out_ref[pl.ds(m * 2 + half, 512, stride=8), :] = high.astype(F32) + low.astype(F32)

        @pl.when(inside & jnp.logical_not(is_panel))
        def _():
            put(value())

        @pl.when(same & jnp.logical_not(is_panel))
        def _():
            here = jnp.where(f == 0, noise[:, :256], noise[:, 256:])
            put(value() + jnp.where(near, here, 0.0))

        @pl.when(jnp.logical_not(inside | same))
        def _():
            put(jnp.zeros((512, 256), F32))


def schur(rows, cols, lead, leadt, w, s):
    return pl.pallas_call(
        schur_kernel,
        grid=(4,),
        out_shape=(
            jax.ShapeDtypeStruct((4 * 512 * 8, 128), F32),
            jax.ShapeDtypeStruct((1, 512), F32),
        ),
        in_specs=[
            pl.BlockSpec((8, 2, None, 64, 512), lambda l: (0, 0, l, 0, 0)),
            VMEM, VMEM, VMEM, VMEM,
            pl.BlockSpec((1, 1, 512), lambda l: (l, 0, 0)),
        ],
        out_specs=(
            pl.BlockSpec((512 * 8, 128), lambda l: (l, 0)),
            pl.BlockSpec((1, 512), lambda l: (0, 0)),
        ),
        scratch_shapes=[
            pltpu.VMEM((512, 1536), BF16),
            pltpu.VMEM((1536, 512), BF16),
            pltpu.VMEM((512, 2560), BF16),
            pltpu.VMEM((4, 2560, 256), BF16),
        ],
        compiler_params=pltpu.CompilerParams(vmem_limit_bytes=VMEM_LIMIT),
        name="schur",
    )(rows, cols, lead, leadt, w, s)


def total_kernel(trace_ref, log_ref, mean_ref, det_ref, slots, own_sem, send, recv):
    a, b = lax.axis_index("x_lo"), lax.axis_index("y")
    own = a * 4 + b

    def peer(d):
        return {"x_lo": (a + d // 4) % 2, "y": (b + d % 4) % 4}

    keep = pltpu.make_async_copy(trace_ref, slots.at[own], own_sem)
    keep.start()
    barrier = pltpu.get_barrier_semaphore()
    for d in range(1, 8):
        pl.semaphore_signal(barrier, inc=1, device_id=peer(d), device_id_type=IDS)
    pl.semaphore_wait(barrier, 7)
    pieces = [remote(trace_ref, slots.at[own], send.at[d - 1], recv.at[own], peer(d)) for d in range(1, 8)]
    for piece in pieces:
        piece.start()
    det_ref[0, 0] = jnp.sum(log_ref[:, 0:1])
    keep.wait()
    for d in range(1, 8):
        q = ((a + d // 4) % 2) * 4 + (b + d % 4) % 4
        pltpu.make_async_copy(slots.at[q], slots.at[q], recv.at[q]).wait()
    mean_ref[0, 0] = jnp.sum(slots[...]) / F32(32 * 512 - 512)
    for piece in pieces:
        piece.wait_send()


def totals(trace, logs):
    dma = pltpu.SemaphoreType.DMA
    scalar = jax.ShapeDtypeStruct((1, 1), F32)
    smem = pl.BlockSpec(memory_space=pltpu.SMEM)
    return pl.pallas_call(
        total_kernel,
        out_shape=(scalar, scalar),
        in_specs=[ANY, VMEM],
        out_specs=(smem, smem),
        scratch_shapes=[pltpu.VMEM((8, 1, 512), F32), dma, dma((7,)), dma((8,))],
        compiler_params=pltpu.CompilerParams(collective_id=1, has_side_effects=True),
        name="totals",
    )(trace, logs)


def shards(points, point_noise):
    x = jnp.swapaxes(points[:, 0], 1, 2)
    s = point_noise.reshape(4, 512)
    rows, cols, lead, leadt, w, logs = gather(x, s.reshape(4, 4, 128))
    out, trace = schur(rows, cols, lead, leadt, w, s.reshape(4, 1, 512))
    mean, det = totals(trace, logs)
    return out.reshape(4, 1, 512, 4, 1, 256), mean.reshape(()), det.reshape(())


def solution(mesh):
    torus = Mesh(mesh.devices.reshape(2, 4, 4, 2, mesh.shape["feat"]), AXES)
    return jax.shard_map(
        shards,
        mesh=torus,
        in_specs=(P(None, ROW, None, ("z", "core", "x_hi")), P(None, ROW, None)),
        out_specs=(P(None, ROW, None, None, COL, "x_hi"), P(), P()),
        check_vma=False,
    )
```

```python
import jax
import jax.numpy as jnp
from jax import lax
from jax.experimental import pallas as pl
from jax.experimental.pallas import tpu as pltpu
from jax.sharding import Mesh
from jax.sharding import PartitionSpec as P

F32 = jnp.float32
BF16 = jnp.bfloat16
HIGHEST = lax.Precision.HIGHEST
IDS = pl.DeviceIdType.MESH
AXES = ("x_lo", "y", "z", "core", "x_hi")
ROW = ("x_lo", "y")
COL = ("z", "core")
VMEM = pl.BlockSpec(memory_space=pltpu.VMEM)
ANY = pl.BlockSpec(memory_space=pl.ANY)
VMEM_LIMIT = 60 * 1024 * 1024


def factor_block(block, hook):
    lane = lax.broadcasted_iota(jnp.int32, (8, 128), 1)
    sub = lax.broadcasted_iota(jnp.int32, (8, 128), 0)
    rows, logs = [], jnp.zeros((8, 128), F32)
    top, below = block[:8], block[8:]
    for k in range(16):
        c, n = 8 * k, 120 - 8 * k
        if k == 8:
            hook()
        diag = [jnp.broadcast_to(top[:, c + t : c + t + 1], (8, 128)) for t in range(8)]
        here = (lane >= c) & (lane < c + 8)
        top = jnp.where(here, jnp.where(lane - c == sub, 1.0, 0.0), top)
        if n:
            cols = [jnp.broadcast_to(below[:, c + t : c + t + 1], (n, 128)) for t in range(8)]
            wide = lax.broadcasted_iota(jnp.int32, (n, 128), 1)
            below = jnp.where((wide >= c) & (wide < c + 8), 0.0, below)
        pivots = jnp.zeros((8, 128), F32)
        for t in range(8):
            pivot = diag[t][t : t + 1, :]
            inv = 1.0 / pivot
            pivots = jnp.where(sub == t, pivot, pivots)
            factor = jnp.where(sub > t, diag[t] * inv, 0.0)
            row = top[t : t + 1, :]
            ends = [diag[j][t : t + 1, :] for j in range(8)]
            for j in range(t + 1, 8):
                diag[j] = diag[j] - factor * ends[j]
            top = top - factor * row
            if n:
                scaled = cols[t] * inv
                below = below - scaled * row
                for j in range(t + 1, 8):
                    cols[j] = cols[j] - scaled * ends[j]
        rows.append(jnp.where(lane < c + 8, top, 0.0) * lax.rsqrt(pivots))
        logs = logs + jnp.log(pivots)
        if n:
            top, below = below[:8], below[8:]
    return jnp.concatenate(rows, 0), logs


def factor_step(k, w_ref, log_ref, hook, between):
    n = w_ref.shape[0]
    at = pl.ds(pl.multiple_of(k * 128, 128), 128)
    block, logs = factor_block(w_ref[at, at], hook)
    log_ref[...] += logs
    between()
    col_block = lax.broadcasted_iota(jnp.int32, (128, n), 1) // 128
    lead = jnp.dot(block, w_ref[at, :], precision=HIGHEST)
    lead = jnp.where(col_block == k, jnp.concatenate([block] * (n // 128), 1), lead)

    @pl.when(k < n // 128 - 1)
    def _():
        row_block = lax.broadcasted_iota(jnp.int32, (n, 128), 0) // 128
        all_block = lax.broadcasted_iota(jnp.int32, (n, n), 1) // 128
        left = lax.dot_general(w_ref[:, at], block, (((1,), (1,)), ((), ())), precision=HIGHEST)
        left = jnp.where(row_block > k, left, 0.0)
        rest = jnp.where(all_block == k, 0.0, w_ref[...])
        w_ref[...] = rest - jnp.dot(left, lead, precision=HIGHEST)

    w_ref[at, :] = lead


def split(value):
    high = value.astype(BF16)
    return high, (value - high.astype(F32)).astype(BF16)


def dot(left, right):
    return jnp.dot(left, right, preferred_element_type=F32)


def remote(src, dst, send, recv, to):
    return pltpu.make_async_remote_copy(
        src_ref=src, dst_ref=dst, send_sem=send, recv_sem=recv, device_id=to, device_id_type=IDS
    )


def gather_kernel(
    x_ref, s_ref,
    points_out, cols_out, panel_out, cross_out, mean_ref, det_ref,
    lead, rows, cols, noise, own_noise, lead_out, w_ref, log_ref, wide, tall, points, panel, cross, slots,
    own_sem, noise_sem, row_out, col_out, trace_send, trace_recv, share_send, share_recv, lead_send, lead_recv, noise_send, noise_recv, line_send, line_recv,
    swap_send, swap_recv, row_send, row_recv, rswap_send, rswap_recv, spread_send, spread_recv, col_send, col_recv,
):
    a, b, z, k, h = (lax.axis_index(name) for name in AXES)
    q_line = z * 2 + h
    partner = {"core": 1 - k}

    def plane(d):
        return {"x_lo": (a + d // 4) % 2, "y": (b + d % 4) % 4}

    def line(d):
        return {"x_hi": (h + d // 4) % 2, "z": (z + d % 4) % 4}

    row_group = a * 4 + b
    to_z, to_k = row_group // 2, row_group % 2
    to_a, to_b = (a + h) % 2, (b + z) % 4
    col_group = z * 2 + k
    from_a, from_b = col_group // 4, col_group % 4

    def spread_to(f):
        return {"x_lo": to_a, "y": to_b, "z": to_z, "core": to_k, "x_hi": f}

    def spread_self(f):
        return (a == to_a) & (b == to_b) & (z == to_z) & (k == to_k) & (h == f)

    def spread_from(kk):
        return {"x_lo": from_a, "y": from_b, "z": (b + 4 - from_b) % 4, "core": kk, "x_hi": (a + from_a) % 2}

    def from_self(kk):
        return (
            (a == from_a) & (b == from_b) & (z == (b + 4 - from_b) % 4) & (k == kk) & (h == (a + from_a) % 2)
        )

    def q_at(da, db):
        return ((b + db + 4 - from_b) % 4) * 2 + (a + da + from_a) % 2

    def q_on(j, db):
        return ((b + db + 4 - from_b) % 4) * 2 + (j + from_a) % 2

    q_plane = q_at(0, 0)

    own_row = pltpu.make_async_copy(x_ref, rows.at[q_line, k], own_sem)
    own_row.start()
    own_s = pltpu.make_async_copy(s_ref, own_noise, noise_sem)
    own_s.start()

    barrier = pltpu.get_barrier_semaphore()
    for d in range(1, 8):
        pl.semaphore_signal(barrier, inc=1, device_id=plane(d), device_id_type=IDS)
        pl.semaphore_signal(barrier, inc=1, device_id=line(d), device_id_type=IDS)
        pl.semaphore_signal(barrier, inc=1, device_id=plane(d) | partner, device_id_type=IDS)
    pl.semaphore_signal(barrier, inc=1, device_id=partner, device_id_type=IDS)
    for i in range(2):
        @pl.when(jnp.logical_not(spread_self(i)))
        def _():
            pl.semaphore_signal(barrier, inc=1, device_id=spread_to(i), device_id_type=IDS)

        @pl.when(jnp.logical_not(from_self(i)))
        def _():
            pl.semaphore_signal(barrier, inc=1, device_id=spread_from(i), device_id_type=IDS)

    selfish = spread_self(0) | spread_self(1)

    @pl.when(selfish)
    def _():
        pl.semaphore_wait(barrier, 24)

    @pl.when(jnp.logical_not(selfish))
    def _():
        pl.semaphore_wait(barrier, 26)

    def row_piece(q, slot, to):
        src = x_ref if slot < 4 else rows.at[q, k]
        return remote(src, rows.at[q, k], row_send.at[slot], row_recv.at[q], to)

    def row_wait(q):
        pltpu.make_async_copy(rows.at[q, k], rows.at[q, k], row_recv.at[q]).wait()

    def col_piece(q, slot, to):
        return remote(cols.at[q], cols.at[q], col_send.at[slot], col_recv.at[q], to)

    def col_wait(q):
        pltpu.make_async_copy(cols.at[q], cols.at[q], col_recv.at[q]).wait()

    put_cols = pltpu.make_async_copy(cols, cols_out, col_out)

    def put_points(l):
        return pltpu.make_async_copy(points.at[l], points_out.at[l], row_out.at[0, l])

    def put_panel(l):
        return pltpu.make_async_copy(panel.at[l], panel_out.at[l], row_out.at[1, l])

    def put_cross(m):
        return pltpu.make_async_copy(cross.at[m], cross_out.at[m], row_out.at[2, m])

    own_slot = row_group * 2 + k

    def trace_piece(d):
        own = slots.at[own_slot]
        to = plane(d % 8) | {"core": (k + d // 8) % 2}
        return remote(own, own, trace_send.at[d - 1], trace_recv.at[own_slot], to)

    def share_piece(j):
        l = k * 2 + j
        return remote(panel.at[l], panel.at[l], share_send.at[j], share_recv.at[l], partner)

    def over_z(d):
        return {"z": (z + d) % 4}

    def over_y(d):
        return {"y": (b + d) % 4}

    q_pair = z * 2 + 1 - h
    q_cross = q_at(1, 0)

    root = b == 0
    source = root & (a == 0)

    def lead_part(q, i):
        return lead.at[q, k, :, pl.ds(128 * i, 128 + 256 * i)]

    def lead_piece(i, d, to):
        dst = lead_part(q_line, i)
        return remote(dst, dst, lead_send.at[i, d], lead_recv.at[i], to)

    def noise_piece(d, to):
        return remote(noise, noise, noise_send.at[d], noise_recv, to)

    @pl.when(source)
    def _():
        for i in range(2):
            given = x_ref.at[0, :, pl.ds(128 * i, 128 + 256 * i)]
            pltpu.make_async_copy(given, lead_part(q_line, i), lead_recv.at[i]).start()
        pltpu.make_async_copy(s_ref.at[0], noise, noise_recv).start()

    def lead_wait(i):
        part = lead_part(q_line, i)
        pltpu.make_async_copy(part, part, lead_recv.at[i]).wait()
        if i == 1:
            pltpu.make_async_copy(noise, noise, noise_recv).wait()

        @pl.when(source)
        def _():
            lead_piece(i, 0, {"x_lo": 1 - a}).start()
            if i == 1:
                noise_piece(0, {"x_lo": 1 - a}).start()

        @pl.when(root)
        def _():
            for d in range(1, 4):
                lead_piece(i, d, {"y": (b + d) % 4}).start()
            if i == 1:
                for d in range(1, 4):
                    noise_piece(d, {"y": (b + d) % 4}).start()

    def spread():
        for f in range(2):
            half = x_ref.at[:, :, f * 256 : f * 256 + 256]
            place = cols.at[q_line, k]

            @pl.when(spread_self(f))
            def _():
                pltpu.make_async_copy(half, place, spread_recv.at[k]).start()

            @pl.when(jnp.logical_not(spread_self(f)))
            def _():
                remote(half, place, spread_send.at[f], spread_recv.at[k], spread_to(f)).start()

    pl.when(jnp.logical_not(root))(spread)
    for d in (1, 3):
        row_piece(q_line, d, over_z(d)).start()

    def line_piece(i, d):
        part = lead_part(q_line, i)
        return remote(part, part, line_send.at[i, d - 1], line_recv.at[i, q_line], line(d))

    for i in range(2):
        lead_wait(i)
        for d in range(1, 8):
            line_piece(i, d).start()
    pl.when(root)(spread)

    def line_wait(i):
        for d in range(1, 8):
            q = ((z + d % 4) % 4) * 2 + (h + d // 4) % 2
            pltpu.make_async_copy(lead_part(q, i), lead_part(q, i), line_recv.at[i, q]).wait()

    def swap_piece(i):
        part = lead.at[:, k, :, pl.ds(128 * i, 128 + 256 * i)]
        return remote(part, part, swap_send.at[i], swap_recv.at[i], partner)

    def swap_wait(i):
        part = lead.at[:, k, :, pl.ds(128 * i, 128 + 256 * i)]
        pltpu.make_async_copy(part, part, swap_recv.at[i]).wait()

    diag = lax.broadcasted_iota(jnp.int32, (128, 128), 0) == lax.broadcasted_iota(jnp.int32, (128, 128), 1)
    log_ref[...] = jnp.zeros_like(log_ref)
    line_wait(0)
    swap_piece(0).start()
    for kk in range(2):
        pltpu.make_async_copy(cols.at[q_plane, kk], cols.at[q_plane, kk], spread_recv.at[kk]).wait()
    col_piece(q_plane, 0, {"x_lo": 1 - a}).start()
    for d in (1, 3, 2):
        col_piece(q_plane, d, over_y(d)).start()
    swap_wait(0)
    some = lead[:, :, :, :128].reshape(1024, 128)
    lead_out[:128, :] = some.T
    w_ref[:128, :128] = dot(lead_out[:128, :], some) + jnp.where(diag, noise[0:1, :], 0.0)

    def middle_first():
        line_wait(1)
        swap_piece(1).start()
        row_piece(q_line, 0, {"x_hi": 1 - h}).start()
        row_piece(q_line, 2, over_z(2)).start()

    def after_first():
        col_wait(q_cross)
        for d in (1, 3, 2):
            col_piece(q_cross, 3 + d, over_y(d)).start()
        own_row.wait()
        own_s.wait()
        swap_wait(1)
        some = lead[:, :, :, 128:].reshape(1024, 384)
        lead_out[128:, :] = some.T
        w_ref[:128, 128:] = dot(lead_out[:128, :], some)
        for i in range(1, 4):
            block = slice(i * 128, i * 128 + 128)
            w_ref[block, :] = dot(lead_out[block, :], lead[...].reshape(1024, 512))
            w_ref[block, block] += jnp.where(diag, noise[i : i + 1, :], 0.0)

    def middle_second():
        row_wait(q_pair)
        for d in (2, 1, 3):
            row_piece(q_pair, 3 + d, over_z(d)).start()

    def middle_last():
        for d in range(1, 4):
            for j in range(2):
                col_wait(q_on(j, d))
        put_cols.start()
        for d in range(1, 4):
            for j in range(2):
                row_wait(((z + d) % 4) * 2 + j)
        remote(rows.at[:, k], rows.at[:, k], rswap_send, rswap_recv, partner).start()

    def step(i, carry):
        def hook():
            pl.when(i == 0)(middle_first)
            pl.when(i == 1)(middle_second)
            pl.when(i == 3)(middle_last)

        factor_step(i, w_ref, log_ref, hook, lambda: pl.when(i == 0)(after_first))
        return carry

    lax.fori_loop(0, 4, step, 0)
    n = w_ref.shape[0]
    lower = lax.broadcasted_iota(jnp.int32, (n, n), 0) >= lax.broadcasted_iota(jnp.int32, (n, n), 1)
    high, low = split(jnp.where(lower, w_ref[...], 0.0))
    wide[:, :512], wide[:, 512:1024], wide[:, 1024:] = high, low, high
    tall[...] = wide[...].T
    det_ref[0, 0] = jnp.sum(log_ref[:, 0:1])
    slots[own_slot] = jnp.zeros((1, 512), F32)

    pltpu.make_async_copy(rows.at[:, k], rows.at[:, k], rswap_recv).wait()

    def row_step(j, carry):
        l = k * 2 + j
        given = rows[:, :, l].reshape(1024, 512).T
        points[l] = given
        first = dot(given, lead[...].reshape(1024, 512))
        corner = (l == 0) & (row_group == 0)
        eye = lax.broadcasted_iota(jnp.int32, (512, 512), 0) == lax.broadcasted_iota(jnp.int32, (512, 512), 1)
        s = jnp.concatenate([own_noise[l, i : i + 1] for i in range(4)], 1)
        first = first + jnp.where(eye & corner, s, 0.0)
        high, low = split(first)
        value = dot(jnp.concatenate([high, high, low], 1), tall[...])
        high, low = split(value)
        panel[l, :, :512], panel[l, :, 512:] = high, low

        @pl.when(jnp.logical_not(corner))
        def _():
            wider = given.astype(F32)
            total = jnp.sum(wider * wider, axis=0, keepdims=True)
            minus = jnp.sum(value * value, axis=0, keepdims=True)
            slots[own_slot] += total[:, :512] + total[:, 512:] + s - minus

        put_points(l).start()
        put_panel(l).start()
        return carry

    lax.fori_loop(0, 2, row_step, 0)

    def other_step(j, carry):
        l = (1 - k) * 2 + j
        points[l] = rows[:, :, l].reshape(1024, 512).T
        put_points(l).start()
        return carry

    share_piece(0).start()
    lax.fori_loop(0, 2, other_step, 0)
    share_piece(1).start()

    def col_step(m):
        high, low = split(dot(lead_out[...], cols[:, :, m].reshape(1024, 256)))
        high, low = split(-dot(wide[...], jnp.concatenate([high, high, low], 0)))
        cross[m, :512], cross[m, 512:] = high, low
        put_cross(m).start()

    col_step(0)
    for d in range(1, 16):
        trace_piece(d).start()
    col_step(1)
    for j in range(2):
        l = (1 - k) * 2 + j
        pltpu.make_async_copy(panel.at[l], panel.at[l], share_recv.at[l]).wait()
        put_panel(l).start()
    col_step(2)
    col_step(3)
    for d in range(1, 16):
        q = (((a + d % 8 // 4) % 2) * 4 + (b + d % 4) % 4) * 2 + (k + d // 8) % 2
        pltpu.make_async_copy(slots.at[q], slots.at[q], trace_recv.at[q]).wait()
    mean_ref[0, 0] = jnp.sum(slots[...]) / F32(32 * 512 - 512)

    for i in range(2):
        @pl.when(source)
        def _():
            lead_piece(i, 0, partner).wait_send()

        @pl.when(root)
        def _():
            for d in range(1, 4):
                lead_piece(i, d, partner).wait_send()

        for d in range(1, 8):
            line_piece(i, d).wait_send()

    @pl.when(source)
    def _():
        noise_piece(0, partner).wait_send()

    @pl.when(root)
    def _():
        for d in range(1, 4):
            noise_piece(d, partner).wait_send()

    for i in range(2):
        swap_piece(i).wait_send()
        share_piece(i).wait_send()
    for i in range(7):
        row_piece(q_line, i, partner).wait_send()
        col_piece(q_plane, i, partner).wait_send()
    for d in range(1, 16):
        trace_piece(d).wait_send()
    for f in range(2):
        @pl.when(jnp.logical_not(spread_self(f)))
        def _():
            half = x_ref.at[:, :, f * 256 : f * 256 + 256]
            remote(half, cols.at[q_line, k], spread_send.at[f], spread_recv.at[k], spread_to(f)).wait_send()

    remote(rows.at[:, k], rows.at[:, k], rswap_send, rswap_recv, partner).wait_send()
    put_cols.wait()
    for j in range(4):
        put_points(j).wait()
        put_panel(j).wait()
        put_cross(j).wait()


def gather(x, s):
    dma = pltpu.SemaphoreType.DMA
    scalar = jax.ShapeDtypeStruct((1, 1), F32)
    smem = pl.BlockSpec(memory_space=pltpu.SMEM)
    return pl.pallas_call(
        gather_kernel,
        out_shape=(
            jax.ShapeDtypeStruct((4, 512, 1024), BF16),
            jax.ShapeDtypeStruct((8, 2, 4, 64, 256), BF16),
            jax.ShapeDtypeStruct((4, 512, 1024), BF16),
            jax.ShapeDtypeStruct((4, 1024, 256), BF16),
            scalar,
            scalar,
        ),
        in_specs=[ANY, ANY],
        out_specs=(ANY, ANY, ANY, ANY, smem, smem),
        scratch_shapes=[
            pltpu.VMEM((8, 2, 64, 512), BF16),
            pltpu.VMEM((8, 2, 4, 64, 512), BF16),
            pltpu.VMEM((8, 2, 4, 64, 256), BF16),
            pltpu.VMEM((4, 128), F32),
            pltpu.VMEM((4, 4, 128), F32),
            pltpu.VMEM((512, 1024), BF16),
            pltpu.VMEM((512, 512), F32),
            pltpu.VMEM((8, 128), F32),
            pltpu.VMEM((512, 1536), BF16),
            pltpu.VMEM((1536, 512), BF16),
            pltpu.VMEM((4, 512, 1024), BF16),
            pltpu.VMEM((4, 512, 1024), BF16),
            pltpu.VMEM((4, 1024, 256), BF16),
            pltpu.VMEM((16, 1, 512), F32),
            dma, dma, dma((3, 4)), dma, dma((15,)), dma((16,)), dma((2,)), dma((4,)),
            dma((2, 4)), dma((2,)), dma((4,)), dma, dma((2, 7)), dma((2, 8)),
            dma((2,)), dma((2,)), dma((7,)), dma((8,)), dma, dma, dma((2,)), dma((2,)), dma((7,)), dma((8,)),
        ],
        compiler_params=pltpu.CompilerParams(
            collective_id=0, has_side_effects=True, vmem_limit_bytes=VMEM_LIMIT
        ),
        name="gather_factor",
    )(x, s)


def schur_kernel(points_ref, cols_ref, panel_ref, cross_ref, s_ref, out_ref):
    l = pl.program_id(0)
    r = lax.axis_index(ROW)
    c = lax.axis_index(COL)
    f = lax.axis_index("x_hi")
    noise = s_ref[0]
    near = lax.broadcasted_iota(jnp.int32, (512, 256), 0) == lax.broadcasted_iota(jnp.int32, (512, 256), 1) + f * 256
    for m in range(4):
        def put(value):
            for half in range(2):
                out_ref[pl.ds(m * 2 + half, 512, stride=8), :] = value[:, half * 128 : half * 128 + 128]

        is_panel = (c == 0) & (m == 0)
        inside = (l > m) | ((l == m) & (r > c))
        same = (l == m) & (r == c)

        def value():
            high = cross_ref[m, :512]
            total = dot(points_ref[...], cols_ref[:, :, m].reshape(1024, 256))
            total = total + dot(panel_ref[...], jnp.concatenate([high, high], 0))
            return total + dot(panel_ref[:, :512], cross_ref[m, 512:])

        @pl.when(is_panel)
        def _():
            for half in range(2):
                high = panel_ref[:, pl.ds(pl.multiple_of(f * 256 + half * 128, 128), 128)]
                low = panel_ref[:, pl.ds(pl.multiple_of(512 + f * 256 + half * 128, 128), 128)]
                out_ref[pl.ds(m * 2 + half, 512, stride=8), :] = high.astype(F32) + low.astype(F32)

        @pl.when(inside & jnp.logical_not(is_panel))
        def _():
            put(value())

        @pl.when(same & jnp.logical_not(is_panel))
        def _():
            here = jnp.where(f == 0, noise[:, :256], noise[:, 256:])
            put(value() + jnp.where(near, here, 0.0))

        @pl.when(jnp.logical_not(inside | same))
        def _():
            put(jnp.zeros((512, 256), F32))


def schur(points, cols, panel, cross, s):
    tile = pl.BlockSpec((None, 512, 1024), lambda l: (l, 0, 0))
    return pl.pallas_call(
        schur_kernel,
        grid=(4,),
        out_shape=jax.ShapeDtypeStruct((4 * 512 * 8, 128), F32),
        in_specs=[tile, VMEM, tile, VMEM, pl.BlockSpec((1, 1, 512), lambda l: (l, 0, 0))],
        out_specs=pl.BlockSpec((512 * 8, 128), lambda l: (l, 0)),
        compiler_params=pltpu.CompilerParams(vmem_limit_bytes=VMEM_LIMIT),
        name="schur",
    )(points, cols, panel, cross, s)


def shards(points, point_noise):
    x = jnp.swapaxes(points[:, 0], 1, 2)
    s = point_noise.reshape(4, 512)
    given, cols, panel, cross, mean, det = gather(x, s.reshape(4, 4, 128))
    out = schur(given, cols, panel, cross, s.reshape(4, 1, 512))
    return out.reshape(4, 1, 512, 4, 1, 256), mean.reshape(()), det.reshape(())


def solution(mesh):
    torus = Mesh(mesh.devices.reshape(2, 4, 4, 2, mesh.shape["feat"]), AXES)
    return jax.shard_map(
        shards,
        mesh=torus,
        in_specs=(P(None, ROW, None, ("z", "core", "x_hi")), P(None, ROW, None)),
        out_specs=(P(None, ROW, None, None, COL, "x_hi"), P(), P()),
        check_vma=False,
    )
```

```python
import jax
import jax.numpy as jnp
from jax import lax
from jax.experimental import pallas as pl
from jax.experimental.pallas import tpu as pltpu
from jax.sharding import Mesh
from jax.sharding import PartitionSpec as P

F32 = jnp.float32
BF16 = jnp.bfloat16
HIGHEST = lax.Precision.HIGHEST
IDS = pl.DeviceIdType.MESH
AXES = ("x_lo", "y", "z", "core", "x_hi")
ROW = ("x_lo", "y")
COL = ("z", "core")
VMEM = pl.BlockSpec(memory_space=pltpu.VMEM)
ANY = pl.BlockSpec(memory_space=pl.ANY)
VMEM_LIMIT = 60 * 1024 * 1024


def factor_block(block, hook):
    lane = lax.broadcasted_iota(jnp.int32, (8, 128), 1)
    sub = lax.broadcasted_iota(jnp.int32, (8, 128), 0)
    rows, logs = [], jnp.zeros((8, 128), F32)
    top, below = block[:8], block[8:]
    for k in range(16):
        c, n = 8 * k, 120 - 8 * k
        if k == 8:
            hook()
        diag = [jnp.broadcast_to(top[:, c + t : c + t + 1], (8, 128)) for t in range(8)]
        here = (lane >= c) & (lane < c + 8)
        top = jnp.where(here, jnp.where(lane - c == sub, 1.0, 0.0), top)
        if n:
            cols = [jnp.broadcast_to(below[:, c + t : c + t + 1], (n, 128)) for t in range(8)]
            wide = lax.broadcasted_iota(jnp.int32, (n, 128), 1)
            below = jnp.where((wide >= c) & (wide < c + 8), 0.0, below)
        pivots = jnp.zeros((8, 128), F32)
        for t in range(8):
            pivot = diag[t][t : t + 1, :]
            inv = 1.0 / pivot
            pivots = jnp.where(sub == t, pivot, pivots)
            factor = jnp.where(sub > t, diag[t] * inv, 0.0)
            row = top[t : t + 1, :]
            ends = [diag[j][t : t + 1, :] for j in range(8)]
            for j in range(t + 1, 8):
                diag[j] = diag[j] - factor * ends[j]
            top = top - factor * row
            if n:
                scaled = cols[t] * inv
                below = below - scaled * row
                for j in range(t + 1, 8):
                    cols[j] = cols[j] - scaled * ends[j]
        rows.append(jnp.where(lane < c + 8, top, 0.0) * lax.rsqrt(pivots))
        logs = logs + jnp.log(pivots)
        if n:
            top, below = below[:8], below[8:]
    return jnp.concatenate(rows, 0), logs


def factor_step(k, w_ref, log_ref, hook, between):
    n = w_ref.shape[0]
    at = pl.ds(pl.multiple_of(k * 128, 128), 128)
    block, logs = factor_block(w_ref[at, at], hook)
    log_ref[...] += logs
    between()
    col_block = lax.broadcasted_iota(jnp.int32, (128, n), 1) // 128
    lead = jnp.dot(block, w_ref[at, :], precision=HIGHEST)
    lead = jnp.where(col_block == k, jnp.concatenate([block] * (n // 128), 1), lead)

    @pl.when(k < n // 128 - 1)
    def _():
        row_block = lax.broadcasted_iota(jnp.int32, (n, 128), 0) // 128
        all_block = lax.broadcasted_iota(jnp.int32, (n, n), 1) // 128
        left = lax.dot_general(w_ref[:, at], block, (((1,), (1,)), ((), ())), precision=HIGHEST)
        left = jnp.where(row_block > k, left, 0.0)
        rest = jnp.where(all_block == k, 0.0, w_ref[...])
        w_ref[...] = rest - jnp.dot(left, lead, precision=HIGHEST)

    w_ref[at, :] = lead


def split(value):
    high = value.astype(BF16)
    return high, (value - high.astype(F32)).astype(BF16)


def dot(left, right):
    return jnp.dot(left, right, preferred_element_type=F32)


def remote(src, dst, send, recv, to):
    return pltpu.make_async_remote_copy(
        src_ref=src, dst_ref=dst, send_sem=send, recv_sem=recv, device_id=to, device_id_type=IDS
    )


def gather_kernel(
    x_ref, s_ref,
    points_out, cols_out, panel_out, cross_out, mean_ref, det_ref,
    lead, rows, cols, noise, own_noise, lead_out, w_ref, log_ref, wide, tall, points, panel, cross, slots,
    own_sem, noise_sem, row_out, col_out, trace_send, trace_recv, share_send, share_recv, lead_send, lead_recv, noise_send, noise_recv, line_send, line_recv,
    swap_send, swap_recv, row_send, row_recv, rswap_send, rswap_recv, spread_send, spread_recv, col_send, col_recv,
):
    a, b, z, k, h = (lax.axis_index(name) for name in AXES)
    q_line = z * 2 + h
    partner = {"core": 1 - k}

    def plane(d):
        return {"x_lo": (a + d // 4) % 2, "y": (b + d % 4) % 4}

    def line(d):
        return {"x_hi": (h + d // 4) % 2, "z": (z + d % 4) % 4}

    row_group = a * 4 + b
    to_z, to_k = row_group // 2, row_group % 2
    to_a, to_b = (a + h) % 2, (b + z) % 4
    col_group = z * 2 + k
    from_a, from_b = col_group // 4, col_group % 4

    def spread_to(f):
        return {"x_lo": to_a, "y": to_b, "z": to_z, "core": to_k, "x_hi": f}

    def spread_self(f):
        return (a == to_a) & (b == to_b) & (z == to_z) & (k == to_k) & (h == f)

    def spread_from(kk):
        return {"x_lo": from_a, "y": from_b, "z": (b + 4 - from_b) % 4, "core": kk, "x_hi": (a + from_a) % 2}

    def from_self(kk):
        return (
            (a == from_a) & (b == from_b) & (z == (b + 4 - from_b) % 4) & (k == kk) & (h == (a + from_a) % 2)
        )

    def q_at(da, db):
        return ((b + db + 4 - from_b) % 4) * 2 + (a + da + from_a) % 2

    def q_on(j, db):
        return ((b + db + 4 - from_b) % 4) * 2 + (j + from_a) % 2

    q_plane = q_at(0, 0)

    own_row = pltpu.make_async_copy(x_ref, rows.at[q_line, k], own_sem)
    own_row.start()
    own_s = pltpu.make_async_copy(s_ref, own_noise, noise_sem)
    own_s.start()

    barrier = pltpu.get_barrier_semaphore()
    for d in range(1, 8):
        pl.semaphore_signal(barrier, inc=1, device_id=plane(d), device_id_type=IDS)
        pl.semaphore_signal(barrier, inc=1, device_id=line(d), device_id_type=IDS)
        pl.semaphore_signal(barrier, inc=1, device_id=plane(d) | partner, device_id_type=IDS)
    pl.semaphore_signal(barrier, inc=1, device_id=partner, device_id_type=IDS)
    for i in range(2):
        @pl.when(jnp.logical_not(spread_self(i)))
        def _():
            pl.semaphore_signal(barrier, inc=1, device_id=spread_to(i), device_id_type=IDS)

        @pl.when(jnp.logical_not(from_self(i)))
        def _():
            pl.semaphore_signal(barrier, inc=1, device_id=spread_from(i), device_id_type=IDS)

    selfish = spread_self(0) | spread_self(1)

    @pl.when(selfish)
    def _():
        pl.semaphore_wait(barrier, 24)

    @pl.when(jnp.logical_not(selfish))
    def _():
        pl.semaphore_wait(barrier, 26)

    def row_piece(q, slot, to):
        src = x_ref if slot < 4 else rows.at[q, k]
        return remote(src, rows.at[q, k], row_send.at[slot], row_recv.at[q], to)

    def row_wait(q):
        pltpu.make_async_copy(rows.at[q, k], rows.at[q, k], row_recv.at[q]).wait()

    def col_piece(q, slot, to):
        return remote(cols.at[q], cols.at[q], col_send.at[slot], col_recv.at[q], to)

    def col_wait(q):
        pltpu.make_async_copy(cols.at[q], cols.at[q], col_recv.at[q]).wait()

    put_cols = pltpu.make_async_copy(cols, cols_out, col_out)

    def put_points(l):
        return pltpu.make_async_copy(points.at[l], points_out.at[l], row_out.at[0, l])

    def put_panel(l):
        return pltpu.make_async_copy(panel.at[l], panel_out.at[l], row_out.at[1, l])

    def put_cross(m):
        return pltpu.make_async_copy(cross.at[m], cross_out.at[m], row_out.at[2, m])

    own_slot = row_group * 2 + k

    def trace_piece(d):
        own = slots.at[own_slot]
        to = plane(d % 8) | {"core": (k + d // 8) % 2}
        return remote(own, own, trace_send.at[d - 1], trace_recv.at[own_slot], to)

    def share_piece(j):
        l = k * 2 + j
        return remote(panel.at[l], panel.at[l], share_send.at[j], share_recv.at[l], partner)

    def over_z(d):
        return {"z": (z + d) % 4}

    def over_y(d):
        return {"y": (b + d) % 4}

    q_pair = z * 2 + 1 - h
    q_cross = q_at(1, 0)

    root = b == 0
    source = root & (a == 0)

    def lead_part(q, i):
        return lead.at[q, k, :, pl.ds(128 * i, 128 + 256 * i)]

    def lead_piece(i, d, to):
        dst = lead_part(q_line, i)
        return remote(dst, dst, lead_send.at[i, d], lead_recv.at[i], to)

    def noise_piece(d, to):
        return remote(noise, noise, noise_send.at[d], noise_recv, to)

    @pl.when(source)
    def _():
        for i in range(2):
            given = x_ref.at[0, :, pl.ds(128 * i, 128 + 256 * i)]
            pltpu.make_async_copy(given, lead_part(q_line, i), lead_recv.at[i]).start()
        pltpu.make_async_copy(s_ref.at[0], noise, noise_recv).start()

    def lead_wait(i):
        part = lead_part(q_line, i)
        pltpu.make_async_copy(part, part, lead_recv.at[i]).wait()
        if i == 1:
            pltpu.make_async_copy(noise, noise, noise_recv).wait()

        @pl.when(source)
        def _():
            lead_piece(i, 0, {"x_lo": 1 - a}).start()
            if i == 1:
                noise_piece(0, {"x_lo": 1 - a}).start()

        @pl.when(root)
        def _():
            for d in range(1, 4):
                lead_piece(i, d, {"y": (b + d) % 4}).start()
            if i == 1:
                for d in range(1, 4):
                    noise_piece(d, {"y": (b + d) % 4}).start()

    def spread():
        for f in range(2):
            half = x_ref.at[:, :, f * 256 : f * 256 + 256]
            place = cols.at[q_line, k]

            @pl.when(spread_self(f))
            def _():
                pltpu.make_async_copy(half, place, spread_recv.at[k]).start()

            @pl.when(jnp.logical_not(spread_self(f)))
            def _():
                remote(half, place, spread_send.at[f], spread_recv.at[k], spread_to(f)).start()

    pl.when(jnp.logical_not(root))(spread)

    def line_piece(i, d):
        part = lead_part(q_line, i)
        return remote(part, part, line_send.at[i, d - 1], line_recv.at[i, q_line], line(d))

    for i in range(2):
        lead_wait(i)
        for d in range(1, 8):
            line_piece(i, d).start()
    pl.when(root)(spread)

    def line_wait(i):
        for d in range(1, 8):
            q = ((z + d % 4) % 4) * 2 + (h + d // 4) % 2
            pltpu.make_async_copy(lead_part(q, i), lead_part(q, i), line_recv.at[i, q]).wait()

    def swap_piece(i):
        part = lead.at[:, k, :, pl.ds(128 * i, 128 + 256 * i)]
        return remote(part, part, swap_send.at[i], swap_recv.at[i], partner)

    def swap_wait(i):
        part = lead.at[:, k, :, pl.ds(128 * i, 128 + 256 * i)]
        pltpu.make_async_copy(part, part, swap_recv.at[i]).wait()

    diag = lax.broadcasted_iota(jnp.int32, (128, 128), 0) == lax.broadcasted_iota(jnp.int32, (128, 128), 1)
    log_ref[...] = jnp.zeros_like(log_ref)
    line_wait(0)
    swap_piece(0).start()
    for d in (1, 3):
        row_piece(q_line, d, over_z(d)).start()
    for kk in range(2):
        pltpu.make_async_copy(cols.at[q_plane, kk], cols.at[q_plane, kk], spread_recv.at[kk]).wait()
    col_piece(q_plane, 0, {"x_lo": 1 - a}).start()
    for d in (1, 3, 2):
        col_piece(q_plane, d, over_y(d)).start()
    swap_wait(0)
    some = lead[:, :, :, :128].reshape(1024, 128)
    lead_out[:128, :] = some.T
    w_ref[:128, :128] = dot(lead_out[:128, :], some) + jnp.where(diag, noise[0:1, :], 0.0)

    def middle_first():
        line_wait(1)
        swap_piece(1).start()
        row_piece(q_line, 0, {"x_hi": 1 - h}).start()
        row_piece(q_line, 2, over_z(2)).start()

    def after_first():
        col_wait(q_cross)
        for d in (1, 3, 2):
            col_piece(q_cross, 3 + d, over_y(d)).start()
        own_row.wait()
        own_s.wait()
        swap_wait(1)
        some = lead[:, :, :, 128:].reshape(1024, 384)
        lead_out[128:, :] = some.T
        w_ref[:128, 128:] = dot(lead_out[:128, :], some)
        for i in range(1, 4):
            block = slice(i * 128, i * 128 + 128)
            w_ref[block, :] = dot(lead_out[block, :], lead[...].reshape(1024, 512))
            w_ref[block, block] += jnp.where(diag, noise[i : i + 1, :], 0.0)

    def middle_second():
        row_wait(q_pair)
        for d in (2, 1, 3):
            row_piece(q_pair, 3 + d, over_z(d)).start()

    def middle_last():
        for d in range(1, 4):
            for j in range(2):
                col_wait(q_on(j, d))
        put_cols.start()
        for d in range(1, 4):
            for j in range(2):
                row_wait(((z + d) % 4) * 2 + j)
        remote(rows.at[:, k], rows.at[:, k], rswap_send, rswap_recv, partner).start()

    def step(i, carry):
        def hook():
            pl.when(i == 0)(middle_first)
            pl.when(i == 1)(middle_second)
            pl.when(i == 3)(middle_last)

        factor_step(i, w_ref, log_ref, hook, lambda: pl.when(i == 0)(after_first))
        return carry

    lax.fori_loop(0, 4, step, 0)
    n = w_ref.shape[0]
    lower = lax.broadcasted_iota(jnp.int32, (n, n), 0) >= lax.broadcasted_iota(jnp.int32, (n, n), 1)
    high, low = split(jnp.where(lower, w_ref[...], 0.0))
    wide[:, :512], wide[:, 512:1024], wide[:, 1024:] = high, low, high
    tall[...] = wide[...].T
    det_ref[0, 0] = jnp.sum(log_ref[:, 0:1])
    slots[own_slot] = jnp.zeros((1, 512), F32)

    pltpu.make_async_copy(rows.at[:, k], rows.at[:, k], rswap_recv).wait()

    def row_step(j, carry):
        l = k * 2 + j
        given = rows[:, :, l].reshape(1024, 512).T
        points[l] = given
        first = dot(given, lead[...].reshape(1024, 512))
        corner = (l == 0) & (row_group == 0)
        eye = lax.broadcasted_iota(jnp.int32, (512, 512), 0) == lax.broadcasted_iota(jnp.int32, (512, 512), 1)
        s = jnp.concatenate([own_noise[l, i : i + 1] for i in range(4)], 1)
        first = first + jnp.where(eye & corner, s, 0.0)
        high, low = split(first)
        value = dot(jnp.concatenate([high, high, low], 1), tall[...])
        high, low = split(value)
        panel[l, :, :512], panel[l, :, 512:] = high, low

        @pl.when(jnp.logical_not(corner))
        def _():
            wider = given.astype(F32)
            total = jnp.sum(wider * wider, axis=0, keepdims=True)
            minus = jnp.sum(value * value, axis=0, keepdims=True)
            slots[own_slot] += total[:, :512] + total[:, 512:] + s - minus

        put_points(l).start()
        put_panel(l).start()
        return carry

    lax.fori_loop(0, 2, row_step, 0)

    def other_step(j, carry):
        l = (1 - k) * 2 + j
        points[l] = rows[:, :, l].reshape(1024, 512).T
        put_points(l).start()
        return carry

    share_piece(0).start()
    lax.fori_loop(0, 2, other_step, 0)
    share_piece(1).start()

    def col_step(m):
        high, low = split(dot(lead_out[...], cols[:, :, m].reshape(1024, 256)))
        high, low = split(-dot(wide[...], jnp.concatenate([high, high, low], 0)))
        cross[m, :512], cross[m, 512:] = high, low
        put_cross(m).start()

    col_step(0)
    for d in range(1, 16):
        trace_piece(d).start()
    col_step(1)
    for j in range(2):
        l = (1 - k) * 2 + j
        pltpu.make_async_copy(panel.at[l], panel.at[l], share_recv.at[l]).wait()
        put_panel(l).start()
    col_step(2)
    col_step(3)
    for d in range(1, 16):
        q = (((a + d % 8 // 4) % 2) * 4 + (b + d % 4) % 4) * 2 + (k + d // 8) % 2
        pltpu.make_async_copy(slots.at[q], slots.at[q], trace_recv.at[q]).wait()
    mean_ref[0, 0] = jnp.sum(slots[...]) / F32(32 * 512 - 512)

    for i in range(2):
        @pl.when(source)
        def _():
            lead_piece(i, 0, partner).wait_send()

        @pl.when(root)
        def _():
            for d in range(1, 4):
                lead_piece(i, d, partner).wait_send()

        for d in range(1, 8):
            line_piece(i, d).wait_send()

    @pl.when(source)
    def _():
        noise_piece(0, partner).wait_send()

    @pl.when(root)
    def _():
        for d in range(1, 4):
            noise_piece(d, partner).wait_send()

    for i in range(2):
        swap_piece(i).wait_send()
        share_piece(i).wait_send()
    for i in range(7):
        row_piece(q_line, i, partner).wait_send()
        col_piece(q_plane, i, partner).wait_send()
    for d in range(1, 16):
        trace_piece(d).wait_send()
    for f in range(2):
        @pl.when(jnp.logical_not(spread_self(f)))
        def _():
            half = x_ref.at[:, :, f * 256 : f * 256 + 256]
            remote(half, cols.at[q_line, k], spread_send.at[f], spread_recv.at[k], spread_to(f)).wait_send()

    remote(rows.at[:, k], rows.at[:, k], rswap_send, rswap_recv, partner).wait_send()
    put_cols.wait()
    for j in range(4):
        put_points(j).wait()
        put_panel(j).wait()
        put_cross(j).wait()


def gather(x, s):
    dma = pltpu.SemaphoreType.DMA
    scalar = jax.ShapeDtypeStruct((1, 1), F32)
    smem = pl.BlockSpec(memory_space=pltpu.SMEM)
    return pl.pallas_call(
        gather_kernel,
        out_shape=(
            jax.ShapeDtypeStruct((4, 512, 1024), BF16),
            jax.ShapeDtypeStruct((8, 2, 4, 64, 256), BF16),
            jax.ShapeDtypeStruct((4, 512, 1024), BF16),
            jax.ShapeDtypeStruct((4, 1024, 256), BF16),
            scalar,
            scalar,
        ),
        in_specs=[ANY, ANY],
        out_specs=(ANY, ANY, ANY, ANY, smem, smem),
        scratch_shapes=[
            pltpu.VMEM((8, 2, 64, 512), BF16),
            pltpu.VMEM((8, 2, 4, 64, 512), BF16),
            pltpu.VMEM((8, 2, 4, 64, 256), BF16),
            pltpu.VMEM((4, 128), F32),
            pltpu.VMEM((4, 4, 128), F32),
            pltpu.VMEM((512, 1024), BF16),
            pltpu.VMEM((512, 512), F32),
            pltpu.VMEM((8, 128), F32),
            pltpu.VMEM((512, 1536), BF16),
            pltpu.VMEM((1536, 512), BF16),
            pltpu.VMEM((4, 512, 1024), BF16),
            pltpu.VMEM((4, 512, 1024), BF16),
            pltpu.VMEM((4, 1024, 256), BF16),
            pltpu.VMEM((16, 1, 512), F32),
            dma, dma, dma((3, 4)), dma, dma((15,)), dma((16,)), dma((2,)), dma((4,)),
            dma((2, 4)), dma((2,)), dma((4,)), dma, dma((2, 7)), dma((2, 8)),
            dma((2,)), dma((2,)), dma((7,)), dma((8,)), dma, dma, dma((2,)), dma((2,)), dma((7,)), dma((8,)),
        ],
        compiler_params=pltpu.CompilerParams(
            collective_id=0, has_side_effects=True, vmem_limit_bytes=VMEM_LIMIT
        ),
        name="gather_factor",
    )(x, s)


def schur_kernel(points_ref, cols_ref, panel_ref, cross_ref, s_ref, out_ref):
    l = pl.program_id(0)
    r = lax.axis_index(ROW)
    c = lax.axis_index(COL)
    f = lax.axis_index("x_hi")
    noise = s_ref[0]
    near = lax.broadcasted_iota(jnp.int32, (512, 256), 0) == lax.broadcasted_iota(jnp.int32, (512, 256), 1) + f * 256
    for m in range(4):
        def put(value):
            for half in range(2):
                out_ref[pl.ds(m * 2 + half, 512, stride=8), :] = value[:, half * 128 : half * 128 + 128]

        is_panel = (c == 0) & (m == 0)
        inside = (l > m) | ((l == m) & (r > c))
        same = (l == m) & (r == c)

        def value():
            high = cross_ref[m, :512]
            total = dot(points_ref[...], cols_ref[:, :, m].reshape(1024, 256))
            total = total + dot(panel_ref[...], jnp.concatenate([high, high], 0))
            return total + dot(panel_ref[:, :512], cross_ref[m, 512:])

        @pl.when(is_panel)
        def _():
            for half in range(2):
                high = panel_ref[:, pl.ds(pl.multiple_of(f * 256 + half * 128, 128), 128)]
                low = panel_ref[:, pl.ds(pl.multiple_of(512 + f * 256 + half * 128, 128), 128)]
                out_ref[pl.ds(m * 2 + half, 512, stride=8), :] = high.astype(F32) + low.astype(F32)

        @pl.when(inside & jnp.logical_not(is_panel))
        def _():
            put(value())

        @pl.when(same & jnp.logical_not(is_panel))
        def _():
            here = jnp.where(f == 0, noise[:, :256], noise[:, 256:])
            put(value() + jnp.where(near, here, 0.0))

        @pl.when(jnp.logical_not(inside | same))
        def _():
            put(jnp.zeros((512, 256), F32))


def schur(points, cols, panel, cross, s):
    tile = pl.BlockSpec((None, 512, 1024), lambda l: (l, 0, 0))
    return pl.pallas_call(
        schur_kernel,
        grid=(4,),
        out_shape=jax.ShapeDtypeStruct((4 * 512 * 8, 128), F32),
        in_specs=[tile, VMEM, tile, VMEM, pl.BlockSpec((1, 1, 512), lambda l: (l, 0, 0))],
        out_specs=pl.BlockSpec((512 * 8, 128), lambda l: (l, 0)),
        compiler_params=pltpu.CompilerParams(vmem_limit_bytes=VMEM_LIMIT),
        name="schur",
    )(points, cols, panel, cross, s)


def shards(points, point_noise):
    x = jnp.swapaxes(points[:, 0], 1, 2)
    s = point_noise.reshape(4, 512)
    given, cols, panel, cross, mean, det = gather(x, s.reshape(4, 4, 128))
    out = schur(given, cols, panel, cross, s.reshape(4, 1, 512))
    return out.reshape(4, 1, 512, 4, 1, 256), mean.reshape(()), det.reshape(())


def solution(mesh):
    torus = Mesh(mesh.devices.reshape(2, 4, 4, 2, mesh.shape["feat"]), AXES)
    return jax.shard_map(
        shards,
        mesh=torus,
        in_specs=(P(None, ROW, None, ("z", "core", "x_hi")), P(None, ROW, None)),
        out_specs=(P(None, ROW, None, None, COL, "x_hi"), P(), P()),
        check_vma=False,
    )
```

```python
import jax
import jax.numpy as jnp
from jax import lax
from jax.experimental import pallas as pl
from jax.experimental.pallas import tpu as pltpu
from jax.sharding import Mesh
from jax.sharding import PartitionSpec as P

F32 = jnp.float32
BF16 = jnp.bfloat16
HIGHEST = lax.Precision.HIGHEST
IDS = pl.DeviceIdType.MESH
AXES = ("x_lo", "y", "z", "core", "x_hi")
ROW = ("x_lo", "y")
COL = ("z", "core")
VMEM = pl.BlockSpec(memory_space=pltpu.VMEM)
ANY = pl.BlockSpec(memory_space=pl.ANY)
VMEM_LIMIT = 60 * 1024 * 1024


def factor_block(block, hook):
    lane = lax.broadcasted_iota(jnp.int32, (8, 128), 1)
    sub = lax.broadcasted_iota(jnp.int32, (8, 128), 0)
    rows, logs = [], jnp.zeros((8, 128), F32)
    top, below = block[:8], block[8:]
    for k in range(16):
        c, n = 8 * k, 120 - 8 * k
        if k == 8:
            hook()
        diag = [jnp.broadcast_to(top[:, c + t : c + t + 1], (8, 128)) for t in range(8)]
        here = (lane >= c) & (lane < c + 8)
        top = jnp.where(here, jnp.where(lane - c == sub, 1.0, 0.0), top)
        if n:
            cols = [jnp.broadcast_to(below[:, c + t : c + t + 1], (n, 128)) for t in range(8)]
            wide = lax.broadcasted_iota(jnp.int32, (n, 128), 1)
            below = jnp.where((wide >= c) & (wide < c + 8), 0.0, below)
        pivots = jnp.zeros((8, 128), F32)
        for t in range(8):
            pivot = diag[t][t : t + 1, :]
            inv = 1.0 / pivot
            pivots = jnp.where(sub == t, pivot, pivots)
            factor = jnp.where(sub > t, diag[t] * inv, 0.0)
            row = top[t : t + 1, :]
            ends = [diag[j][t : t + 1, :] for j in range(8)]
            for j in range(t + 1, 8):
                diag[j] = diag[j] - factor * ends[j]
            top = top - factor * row
            if n:
                scaled = cols[t] * inv
                below = below - scaled * row
                for j in range(t + 1, 8):
                    cols[j] = cols[j] - scaled * ends[j]
        rows.append(jnp.where(lane < c + 8, top, 0.0) * lax.rsqrt(pivots))
        logs = logs + jnp.log(pivots)
        if n:
            top, below = below[:8], below[8:]
    return jnp.concatenate(rows, 0), logs


def factor_step(k, w_ref, log_ref, hook, between):
    n = w_ref.shape[0]
    at = pl.ds(pl.multiple_of(k * 128, 128), 128)
    block, logs = factor_block(w_ref[at, at], hook)
    log_ref[...] += logs
    between()
    col_block = lax.broadcasted_iota(jnp.int32, (128, n), 1) // 128
    lead = jnp.dot(block, w_ref[at, :], precision=HIGHEST)
    lead = jnp.where(col_block == k, jnp.concatenate([block] * (n // 128), 1), lead)

    @pl.when(k < n // 128 - 1)
    def _():
        row_block = lax.broadcasted_iota(jnp.int32, (n, 128), 0) // 128
        all_block = lax.broadcasted_iota(jnp.int32, (n, n), 1) // 128
        left = lax.dot_general(w_ref[:, at], block, (((1,), (1,)), ((), ())), precision=HIGHEST)
        left = jnp.where(row_block > k, left, 0.0)
        rest = jnp.where(all_block == k, 0.0, w_ref[...])
        w_ref[...] = rest - jnp.dot(left, lead, precision=HIGHEST)

    w_ref[at, :] = lead


def split(value):
    high = value.astype(BF16)
    return high, (value - high.astype(F32)).astype(BF16)


def dot(left, right):
    return jnp.dot(left, right, preferred_element_type=F32)


def remote(src, dst, send, recv, to):
    return pltpu.make_async_remote_copy(
        src_ref=src, dst_ref=dst, send_sem=send, recv_sem=recv, device_id=to, device_id_type=IDS
    )


def gather_kernel(
    x_ref, s_ref,
    points_out, cols_out, panel_out, cross_out, mean_ref, det_ref,
    lead, rows, cols, noise, own_noise, lead_out, w_ref, log_ref, wide, tall, points, panel, cross, slots,
    own_sem, noise_sem, row_out, col_out, trace_send, trace_recv, share_send, share_recv, lead_send, lead_recv, noise_send, noise_recv, line_send, line_recv,
    swap_send, swap_recv, row_send, row_recv, rswap_send, rswap_recv, spread_send, spread_recv, col_send, col_recv,
):
    a, b, z, k, h = (lax.axis_index(name) for name in AXES)
    q_line = z * 2 + h
    partner = {"core": 1 - k}

    def plane(d):
        return {"x_lo": (a + d // 4) % 2, "y": (b + d % 4) % 4}

    def line(d):
        return {"x_hi": (h + d // 4) % 2, "z": (z + d % 4) % 4}

    row_group = a * 4 + b
    to_z, to_k = row_group // 2, row_group % 2
    to_a, to_b = (a + h) % 2, (b + z) % 4
    col_group = z * 2 + k
    from_a, from_b = col_group // 4, col_group % 4

    def spread_to(f):
        return {"x_lo": to_a, "y": to_b, "z": to_z, "core": to_k, "x_hi": f}

    def spread_self(f):
        return (a == to_a) & (b == to_b) & (z == to_z) & (k == to_k) & (h == f)

    def spread_from(kk):
        return {"x_lo": from_a, "y": from_b, "z": (b + 4 - from_b) % 4, "core": kk, "x_hi": (a + from_a) % 2}

    def from_self(kk):
        return (
            (a == from_a) & (b == from_b) & (z == (b + 4 - from_b) % 4) & (k == kk) & (h == (a + from_a) % 2)
        )

    def q_at(da, db):
        return ((b + db + 4 - from_b) % 4) * 2 + (a + da + from_a) % 2

    def q_on(j, db):
        return ((b + db + 4 - from_b) % 4) * 2 + (j + from_a) % 2

    q_plane = q_at(0, 0)

    own_row = pltpu.make_async_copy(x_ref, rows.at[q_line, k], own_sem)
    own_row.start()
    own_s = pltpu.make_async_copy(s_ref, own_noise, noise_sem)
    own_s.start()

    barrier = pltpu.get_barrier_semaphore()
    for d in range(1, 8):
        pl.semaphore_signal(barrier, inc=1, device_id=plane(d), device_id_type=IDS)
        pl.semaphore_signal(barrier, inc=1, device_id=line(d), device_id_type=IDS)
        pl.semaphore_signal(barrier, inc=1, device_id=plane(d) | partner, device_id_type=IDS)
    pl.semaphore_signal(barrier, inc=1, device_id=partner, device_id_type=IDS)
    for i in range(2):
        @pl.when(jnp.logical_not(spread_self(i)))
        def _():
            pl.semaphore_signal(barrier, inc=1, device_id=spread_to(i), device_id_type=IDS)

        @pl.when(jnp.logical_not(from_self(i)))
        def _():
            pl.semaphore_signal(barrier, inc=1, device_id=spread_from(i), device_id_type=IDS)

    selfish = spread_self(0) | spread_self(1)

    @pl.when(selfish)
    def _():
        pl.semaphore_wait(barrier, 24)

    @pl.when(jnp.logical_not(selfish))
    def _():
        pl.semaphore_wait(barrier, 26)

    def row_piece(q, slot, to):
        src = x_ref if slot < 4 else rows.at[q, k]
        return remote(src, rows.at[q, k], row_send.at[slot], row_recv.at[q], to)

    def row_wait(q):
        pltpu.make_async_copy(rows.at[q, k], rows.at[q, k], row_recv.at[q]).wait()

    def col_piece(q, slot, to):
        return remote(cols.at[q], cols.at[q], col_send.at[slot], col_recv.at[q], to)

    def col_wait(q):
        pltpu.make_async_copy(cols.at[q], cols.at[q], col_recv.at[q]).wait()

    put_cols = pltpu.make_async_copy(cols, cols_out, col_out)

    def put_points(l):
        return pltpu.make_async_copy(points.at[l], points_out.at[l], row_out.at[0, l])

    def put_panel(l):
        return pltpu.make_async_copy(panel.at[l], panel_out.at[l], row_out.at[1, l])

    def put_cross(m):
        return pltpu.make_async_copy(cross.at[m], cross_out.at[m], row_out.at[2, m])

    own_slot = row_group * 2 + k

    def trace_piece(d):
        own = slots.at[own_slot]
        to = plane(d % 8) | {"core": (k + d // 8) % 2}
        return remote(own, own, trace_send.at[d - 1], trace_recv.at[own_slot], to)

    def share_piece(j):
        l = k * 2 + j
        return remote(panel.at[l], panel.at[l], share_send.at[j], share_recv.at[l], partner)

    def over_z(d):
        return {"z": (z + d) % 4}

    def over_y(d):
        return {"y": (b + d) % 4}

    q_pair = z * 2 + 1 - h
    q_cross = q_at(1, 0)

    root = b == 0
    source = root & (a == 0)

    def lead_part(q, i):
        return lead.at[q, k, :, pl.ds(128 * i, 128 + 256 * i)]

    def lead_piece(i, d, to):
        dst = lead_part(q_line, i)
        return remote(dst, dst, lead_send.at[i, d], lead_recv.at[i], to)

    def noise_piece(d, to):
        return remote(noise, noise, noise_send.at[d], noise_recv, to)

    @pl.when(source)
    def _():
        for i in range(2):
            given = x_ref.at[0, :, pl.ds(128 * i, 128 + 256 * i)]
            pltpu.make_async_copy(given, lead_part(q_line, i), lead_recv.at[i]).start()
        pltpu.make_async_copy(s_ref.at[0], noise, noise_recv).start()

    def lead_wait(i):
        part = lead_part(q_line, i)
        pltpu.make_async_copy(part, part, lead_recv.at[i]).wait()
        if i == 1:
            pltpu.make_async_copy(noise, noise, noise_recv).wait()

        @pl.when(source)
        def _():
            lead_piece(i, 0, {"x_lo": 1 - a}).start()
            if i == 1:
                noise_piece(0, {"x_lo": 1 - a}).start()

        @pl.when(root)
        def _():
            for d in range(1, 4):
                lead_piece(i, d, {"y": (b + d) % 4}).start()
            if i == 1:
                for d in range(1, 4):
                    noise_piece(d, {"y": (b + d) % 4}).start()

    def spread():
        for f in range(2):
            half = x_ref.at[:, :, f * 256 : f * 256 + 256]
            place = cols.at[q_line, k]

            @pl.when(spread_self(f))
            def _():
                pltpu.make_async_copy(half, place, spread_recv.at[k]).start()

            @pl.when(jnp.logical_not(spread_self(f)))
            def _():
                remote(half, place, spread_send.at[f], spread_recv.at[k], spread_to(f)).start()

    pl.when(jnp.logical_not(root))(spread)

    def line_piece(i, d):
        part = lead_part(q_line, i)
        return remote(part, part, line_send.at[i, d - 1], line_recv.at[i, q_line], line(d))

    for i in range(2):
        lead_wait(i)
        for d in range(1, 8):
            line_piece(i, d).start()
    pl.when(root)(spread)

    def line_wait(i):
        for d in range(1, 8):
            q = ((z + d % 4) % 4) * 2 + (h + d // 4) % 2
            pltpu.make_async_copy(lead_part(q, i), lead_part(q, i), line_recv.at[i, q]).wait()

    def swap_piece(i):
        part = lead.at[:, k, :, pl.ds(128 * i, 128 + 256 * i)]
        return remote(part, part, swap_send.at[i], swap_recv.at[i], partner)

    def swap_wait(i):
        part = lead.at[:, k, :, pl.ds(128 * i, 128 + 256 * i)]
        pltpu.make_async_copy(part, part, swap_recv.at[i]).wait()

    diag = lax.broadcasted_iota(jnp.int32, (128, 128), 0) == lax.broadcasted_iota(jnp.int32, (128, 128), 1)
    log_ref[...] = jnp.zeros_like(log_ref)
    line_wait(0)
    swap_piece(0).start()
    for d in (1, 3):
        row_piece(q_line, d, over_z(d)).start()
    for kk in range(2):
        pltpu.make_async_copy(cols.at[q_plane, kk], cols.at[q_plane, kk], spread_recv.at[kk]).wait()
    col_piece(q_plane, 0, {"x_lo": 1 - a}).start()
    for d in (1, 3):
        col_piece(q_plane, d, over_y(d)).start()
    swap_wait(0)
    some = lead[:, :, :, :128].reshape(1024, 128)
    lead_out[:128, :] = some.T
    w_ref[:128, :128] = dot(lead_out[:128, :], some) + jnp.where(diag, noise[0:1, :], 0.0)

    def middle_first():
        line_wait(1)
        swap_piece(1).start()
        row_piece(q_line, 0, {"x_hi": 1 - h}).start()
        row_piece(q_line, 2, over_z(2)).start()

    def after_first():
        col_wait(q_cross)
        col_piece(q_plane, 2, over_y(2)).start()
        for d in (1, 3, 2):
            col_piece(q_cross, 3 + d, over_y(d)).start()
        own_row.wait()
        own_s.wait()
        swap_wait(1)
        some = lead[:, :, :, 128:].reshape(1024, 384)
        lead_out[128:, :] = some.T
        w_ref[:128, 128:] = dot(lead_out[:128, :], some)
        for i in range(1, 4):
            block = slice(i * 128, i * 128 + 128)
            w_ref[block, :] = dot(lead_out[block, :], lead[...].reshape(1024, 512))
            w_ref[block, block] += jnp.where(diag, noise[i : i + 1, :], 0.0)

    def middle_second():
        row_wait(q_pair)
        for d in (2, 1, 3):
            row_piece(q_pair, 3 + d, over_z(d)).start()

    def middle_last():
        for d in range(1, 4):
            for j in range(2):
                col_wait(q_on(j, d))
        put_cols.start()
        for d in range(1, 4):
            for j in range(2):
                row_wait(((z + d) % 4) * 2 + j)
        for i in range(2):
            row_swap(i).start()

    def row_swap(i):
        part = rows.at[:, k, pl.ds(2 * ((1 - k + i) % 2), 2)]
        return remote(part, part, rswap_send.at[i], rswap_recv.at[i], partner)

    def row_swap_wait(i):
        part = rows.at[:, k, pl.ds(2 * ((k + i) % 2), 2)]
        pltpu.make_async_copy(part, part, rswap_recv.at[i]).wait()

    def step(i, carry):
        def hook():
            pl.when(i == 0)(middle_first)
            pl.when(i == 1)(middle_second)
            pl.when(i == 3)(middle_last)

        factor_step(i, w_ref, log_ref, hook, lambda: pl.when(i == 0)(after_first))
        return carry

    lax.fori_loop(0, 4, step, 0)
    n = w_ref.shape[0]
    lower = lax.broadcasted_iota(jnp.int32, (n, n), 0) >= lax.broadcasted_iota(jnp.int32, (n, n), 1)
    high, low = split(jnp.where(lower, w_ref[...], 0.0))
    wide[:, :512], wide[:, 512:1024], wide[:, 1024:] = high, low, high
    tall[...] = wide[...].T
    det_ref[0, 0] = jnp.sum(log_ref[:, 0:1])
    slots[own_slot] = jnp.zeros((1, 512), F32)

    row_swap_wait(0)

    def row_step(j, carry):
        l = k * 2 + j
        given = rows[:, :, l].reshape(1024, 512).T
        points[l] = given
        first = dot(given, lead[...].reshape(1024, 512))
        corner = (l == 0) & (row_group == 0)
        eye = lax.broadcasted_iota(jnp.int32, (512, 512), 0) == lax.broadcasted_iota(jnp.int32, (512, 512), 1)
        s = jnp.concatenate([own_noise[l, i : i + 1] for i in range(4)], 1)
        first = first + jnp.where(eye & corner, s, 0.0)
        high, low = split(first)
        value = dot(jnp.concatenate([high, high, low], 1), tall[...])
        high, low = split(value)
        panel[l, :, :512], panel[l, :, 512:] = high, low

        @pl.when(jnp.logical_not(corner))
        def _():
            wider = given.astype(F32)
            total = jnp.sum(wider * wider, axis=0, keepdims=True)
            minus = jnp.sum(value * value, axis=0, keepdims=True)
            slots[own_slot] += total[:, :512] + total[:, 512:] + s - minus

        put_points(l).start()
        put_panel(l).start()
        return carry

    lax.fori_loop(0, 2, row_step, 0)

    def other_step(j, carry):
        l = (1 - k) * 2 + j
        points[l] = rows[:, :, l].reshape(1024, 512).T
        put_points(l).start()
        return carry

    share_piece(0).start()
    row_swap_wait(1)
    lax.fori_loop(0, 2, other_step, 0)
    share_piece(1).start()

    def col_step(m):
        high, low = split(dot(lead_out[...], cols[:, :, m].reshape(1024, 256)))
        high, low = split(-dot(wide[...], jnp.concatenate([high, high, low], 0)))
        cross[m, :512], cross[m, 512:] = high, low
        put_cross(m).start()

    col_step(0)
    for d in range(1, 16):
        trace_piece(d).start()
    col_step(1)
    for j in range(2):
        l = (1 - k) * 2 + j
        pltpu.make_async_copy(panel.at[l], panel.at[l], share_recv.at[l]).wait()
        put_panel(l).start()
    col_step(2)
    col_step(3)
    for d in range(1, 16):
        q = (((a + d % 8 // 4) % 2) * 4 + (b + d % 4) % 4) * 2 + (k + d // 8) % 2
        pltpu.make_async_copy(slots.at[q], slots.at[q], trace_recv.at[q]).wait()
    mean_ref[0, 0] = jnp.sum(slots[...]) / F32(32 * 512 - 512)

    for i in range(2):
        @pl.when(source)
        def _():
            lead_piece(i, 0, partner).wait_send()

        @pl.when(root)
        def _():
            for d in range(1, 4):
                lead_piece(i, d, partner).wait_send()

        for d in range(1, 8):
            line_piece(i, d).wait_send()

    @pl.when(source)
    def _():
        noise_piece(0, partner).wait_send()

    @pl.when(root)
    def _():
        for d in range(1, 4):
            noise_piece(d, partner).wait_send()

    for i in range(2):
        swap_piece(i).wait_send()
        share_piece(i).wait_send()
    for i in range(7):
        row_piece(q_line, i, partner).wait_send()
        col_piece(q_plane, i, partner).wait_send()
    for d in range(1, 16):
        trace_piece(d).wait_send()
    for f in range(2):
        @pl.when(jnp.logical_not(spread_self(f)))
        def _():
            half = x_ref.at[:, :, f * 256 : f * 256 + 256]
            remote(half, cols.at[q_line, k], spread_send.at[f], spread_recv.at[k], spread_to(f)).wait_send()

    for i in range(2):
        row_swap(i).wait_send()
    put_cols.wait()
    for j in range(4):
        put_points(j).wait()
        put_panel(j).wait()
        put_cross(j).wait()


def gather(x, s):
    dma = pltpu.SemaphoreType.DMA
    scalar = jax.ShapeDtypeStruct((1, 1), F32)
    smem = pl.BlockSpec(memory_space=pltpu.SMEM)
    return pl.pallas_call(
        gather_kernel,
        out_shape=(
            jax.ShapeDtypeStruct((4, 512, 1024), BF16),
            jax.ShapeDtypeStruct((8, 2, 4, 64, 256), BF16),
            jax.ShapeDtypeStruct((4, 512, 1024), BF16),
            jax.ShapeDtypeStruct((4, 1024, 256), BF16),
            scalar,
            scalar,
        ),
        in_specs=[ANY, ANY],
        out_specs=(ANY, ANY, ANY, ANY, smem, smem),
        scratch_shapes=[
            pltpu.VMEM((8, 2, 64, 512), BF16),
            pltpu.VMEM((8, 2, 4, 64, 512), BF16),
            pltpu.VMEM((8, 2, 4, 64, 256), BF16),
            pltpu.VMEM((4, 128), F32),
            pltpu.VMEM((4, 4, 128), F32),
            pltpu.VMEM((512, 1024), BF16),
            pltpu.VMEM((512, 512), F32),
            pltpu.VMEM((8, 128), F32),
            pltpu.VMEM((512, 1536), BF16),
            pltpu.VMEM((1536, 512), BF16),
            pltpu.VMEM((4, 512, 1024), BF16),
            pltpu.VMEM((4, 512, 1024), BF16),
            pltpu.VMEM((4, 1024, 256), BF16),
            pltpu.VMEM((16, 1, 512), F32),
            dma, dma, dma((3, 4)), dma, dma((15,)), dma((16,)), dma((2,)), dma((4,)),
            dma((2, 4)), dma((2,)), dma((4,)), dma, dma((2, 7)), dma((2, 8)),
            dma((2,)), dma((2,)), dma((7,)), dma((8,)), dma((2,)), dma((2,)), dma((2,)), dma((2,)), dma((7,)), dma((8,)),
        ],
        compiler_params=pltpu.CompilerParams(
            collective_id=0, has_side_effects=True, vmem_limit_bytes=VMEM_LIMIT
        ),
        name="gather_factor",
    )(x, s)


def schur_kernel(points_ref, cols_ref, panel_ref, cross_ref, s_ref, out_ref):
    l = pl.program_id(0)
    r = lax.axis_index(ROW)
    c = lax.axis_index(COL)
    f = lax.axis_index("x_hi")
    noise = s_ref[0]
    near = lax.broadcasted_iota(jnp.int32, (512, 256), 0) == lax.broadcasted_iota(jnp.int32, (512, 256), 1) + f * 256
    for m in range(4):
        def put(value):
            for half in range(2):
                out_ref[pl.ds(m * 2 + half, 512, stride=8), :] = value[:, half * 128 : half * 128 + 128]

        is_panel = (c == 0) & (m == 0)
        inside = (l > m) | ((l == m) & (r > c))
        same = (l == m) & (r == c)

        def value():
            high = cross_ref[m, :512]
            total = dot(points_ref[...], cols_ref[:, :, m].reshape(1024, 256))
            total = total + dot(panel_ref[...], jnp.concatenate([high, high], 0))
            return total + dot(panel_ref[:, :512], cross_ref[m, 512:])

        @pl.when(is_panel)
        def _():
            for half in range(2):
                high = panel_ref[:, pl.ds(pl.multiple_of(f * 256 + half * 128, 128), 128)]
                low = panel_ref[:, pl.ds(pl.multiple_of(512 + f * 256 + half * 128, 128), 128)]
                out_ref[pl.ds(m * 2 + half, 512, stride=8), :] = high.astype(F32) + low.astype(F32)

        @pl.when(inside & jnp.logical_not(is_panel))
        def _():
            put(value())

        @pl.when(same & jnp.logical_not(is_panel))
        def _():
            here = jnp.where(f == 0, noise[:, :256], noise[:, 256:])
            put(value() + jnp.where(near, here, 0.0))

        @pl.when(jnp.logical_not(inside | same))
        def _():
            put(jnp.zeros((512, 256), F32))


def schur(points, cols, panel, cross, s):
    tile = pl.BlockSpec((None, 512, 1024), lambda l: (l, 0, 0))
    return pl.pallas_call(
        schur_kernel,
        grid=(4,),
        out_shape=jax.ShapeDtypeStruct((4 * 512 * 8, 128), F32),
        in_specs=[tile, VMEM, tile, VMEM, pl.BlockSpec((1, 1, 512), lambda l: (l, 0, 0))],
        out_specs=pl.BlockSpec((512 * 8, 128), lambda l: (l, 0)),
        compiler_params=pltpu.CompilerParams(vmem_limit_bytes=VMEM_LIMIT),
        name="schur",
    )(points, cols, panel, cross, s)


def shards(points, point_noise):
    x = jnp.swapaxes(points[:, 0], 1, 2)
    s = point_noise.reshape(4, 512)
    given, cols, panel, cross, mean, det = gather(x, s.reshape(4, 4, 128))
    out = schur(given, cols, panel, cross, s.reshape(4, 1, 512))
    return out.reshape(4, 1, 512, 4, 1, 256), mean.reshape(()), det.reshape(())


def solution(mesh):
    torus = Mesh(mesh.devices.reshape(2, 4, 4, 2, mesh.shape["feat"]), AXES)
    return jax.shard_map(
        shards,
        mesh=torus,
        in_specs=(P(None, ROW, None, ("z", "core", "x_hi")), P(None, ROW, None)),
        out_specs=(P(None, ROW, None, None, COL, "x_hi"), P(), P()),
        check_vma=False,
    )
```
